1024 devices in a mesh: dom: 16 (over x, core), bucket: 64 (over y, z).
Axes of the slice: x: 8, y: 8, z: 8, core: 2. Of those that a mesh axis runs over, the one named last changes fastest.
Arguments:
- emb_table: float32 [262144, 400], P(('dom', 'bucket')), may hold values from -1.6 to 1.6
- rel_diag: float32 [256, 400], replicated, may hold values from 0.5 to 1.5
- send_rows: int32 [16, 64, 16, 32], P('dom', 'bucket'), may hold values from -1 to 255, as said below
- src_slot: int32 [16, 64, 256], P('dom', 'bucket'), may hold values from 0 to 511, as said below
- dst_slot: int32 [16, 64, 256], P('dom', 'bucket'), may hold values from 0 to 511, as said below
- neg_rows: int32 [16, 64, 2, 2], P('dom', 'bucket'), may hold values from 0 to 255
- block_rel: int32 [16, 64, 2], P('dom', 'bucket'), may hold values from 0 to 255
Outputs:
- emb_grad: float32 [262144, 400], P(('dom', 'bucket'))
The draws below stay inside these ranges and needn't reach their ends.
Inputs may be any that keep to these rules, and one draw needn't show every extreme that they name: `send_rows`: entries of one owner, column and bucket device are live (not -1) for slots 0 to some count - 1 and -1 after; at most 32 live rows go from one owner to one bucket device, and every owner fills all 32 slots for some bucket device of its column. `src_slot`: every edge's source slot is a live slot of the received rows. `dst_slot`: every edge's destination slot is a live slot of the received rows.
All inputs are finite; a program needn't handle non-finite values.
Results may differ from the reference program's by a relative error of at most 0.0003.
Values sent between devices are 32-bit elements; how exact they have to be, the bound alone decides.
No kernel may reach another device: no remote copies, remote signals or barrier semaphores. Data moves between devices by JAX's collectives and lax.ppermute only.
A program may use at most 32 MiB of HBM per device.

```python
import jax
import jax.numpy as jnp
from jax import lax

D = 400
ENT_DEV = 256
NREL = 256
SLOT = 32
BLOCKS = 2
OWNERS = 16
COLUMNS = 64
NEG_DEV = 2
EDGES = 256


def layout(key):
    base_key = jax.random.fold_in(key, 5)
    key_a, key_b, key_c, key_d = jax.random.split(base_key, 4)
    lowest = max(1, SLOT // 2)
    counts = jax.random.randint(key_a, (OWNERS, COLUMNS, OWNERS), lowest, SLOT + 1)
    sender = jnp.arange(OWNERS)[:, None, None]
    column = jnp.arange(COLUMNS)[None, :, None]
    receiver = jnp.arange(OWNERS)[None, None, :]
    counts = jnp.where(receiver == (sender + column) % OWNERS, SLOT, counts)
    picks = jax.random.randint(key_b, (OWNERS, COLUMNS, OWNERS, SLOT), 0, ENT_DEV)
    position = jnp.arange(SLOT)
    send_list = jnp.where(position < counts[..., None], picks, -1)
    per_receiver = jnp.transpose(counts, (2, 1, 0))
    owner_pick = jax.random.randint(key_c, (OWNERS, COLUMNS, EDGES, 2), 0, OWNERS)
    dom_ids = jnp.arange(OWNERS)[:, None, None, None]
    col_ids = jnp.arange(COLUMNS)[None, :, None, None]
    limit = per_receiver[dom_ids, col_ids, owner_pick]
    offset = jax.random.randint(key_d, (OWNERS, COLUMNS, EDGES, 2), 0, 1 << 20) % limit
    slots = owner_pick * SLOT + offset
    full_owner = (jnp.arange(OWNERS)[:, None] - jnp.arange(COLUMNS)[None, :]) % OWNERS
    edge_pos = jnp.arange(EDGES)[None, None, :]
    first_slot = (full_owner * SLOT + SLOT - 1)[:, :, None]
    second_slot = (full_owner * SLOT)[:, :, None]
    sources = jnp.where(edge_pos == 0, first_slot, jnp.where(edge_pos == 1, second_slot, slots[..., 0]))
    targets = slots[..., 1]
    return (send_list.astype(jnp.int32), sources.astype(jnp.int32), targets.astype(jnp.int32))


def draw_send_rows(key, part):
    return layout(key)[0]


def draw_src_slot(key, part):
    return layout(key)[1]


def draw_dst_slot(key, part):
    return layout(key)[2]


def draw_emb_table(key, part):
    rows_all = ENT_DEV * OWNERS * COLUMNS
    key_a = jax.random.fold_in(jax.random.fold_in(key, 11), 0)
    values = jnp.clip(0.35 * jax.random.normal(key_a, (rows_all, D)), -1.6, 1.6)
    return values.astype(jnp.float32)


def place_ends(values, rng, low, high):
    shape = values.shape
    spot = [jax.random.randint(jax.random.fold_in(rng, axis), (), 0, shape[axis]) for axis in range(len(shape))]
    values = values.at[tuple(spot)].set(low)
    longest = shape.index(max(shape))
    spot[longest] = (spot[longest] + 1) % shape[longest]
    return values.at[tuple(spot)].set(high)


def setup_inputs(seed: int = 0) -> dict:
    arg_keys = jax.random.split(jax.random.key(seed), 8)
    return {
        "emb_table": draw_emb_table(jax.random.fold_in(arg_keys[7], 71), 0),
        "rel_diag": jnp.clip(jax.random.uniform(arg_keys[1], (NREL, D), jnp.float32, 0.5, 1.5), 0.5, 1.5),
        "send_rows": draw_send_rows(jax.random.fold_in(arg_keys[7], 71), 0),
        "src_slot": draw_src_slot(jax.random.fold_in(arg_keys[7], 71), 0),
        "dst_slot": draw_dst_slot(jax.random.fold_in(arg_keys[7], 71), 0),
        "neg_rows": place_ends(jax.random.randint(arg_keys[5], (OWNERS, COLUMNS, BLOCKS, NEG_DEV), 0, ENT_DEV), jax.random.fold_in(arg_keys[5], 1), 0, ENT_DEV - 1).astype(jnp.int32),
        "block_rel": place_ends(jax.random.randint(arg_keys[6], (OWNERS, COLUMNS, BLOCKS), 0, NREL), jax.random.fold_in(arg_keys[6], 1), 0, NREL - 1).astype(jnp.int32),
    }


def block_grads(sources, targets, negatives, relation):
    highest = lax.Precision.HIGHEST
    query = sources * relation
    positive = jnp.sum(query * targets, axis=-1)
    scores = jnp.einsum("cek,cjk->cej", query, negatives, precision=highest)
    largest = jnp.maximum(jnp.max(scores, axis=-1), positive)
    pos_exp = jnp.exp(positive - largest)
    neg_exp = jnp.exp(scores - largest[..., None])
    total = pos_exp + jnp.sum(neg_exp, axis=-1)
    pos_weight = pos_exp / total - 1.0
    neg_weight = neg_exp / total[..., None]
    query_grad = pos_weight[..., None] * targets + jnp.einsum("cej,cjk->cek", neg_weight, negatives, precision=highest)
    neg_grad = jnp.einsum("cej,cek->cjk", neg_weight, query, precision=highest)
    return query_grad * relation, pos_weight[..., None] * query, neg_grad


def reference(emb_table, rel_diag, send_rows, src_slot, dst_slot, neg_rows, block_rel):
    owners = send_rows.shape[0]
    columns = send_rows.shape[1]
    slot_cap = send_rows.shape[3]
    width = emb_table.shape[1]
    ent_rows = emb_table.shape[0]
    ent_dev = ent_rows // (owners * columns)
    blocks = block_rel.shape[2]
    owner_ids = jnp.arange(owners, dtype=jnp.int32)
    column_ids = jnp.arange(columns, dtype=jnp.int32)

    def device_step(total_grad, device):
        dom_idx = device // columns
        col_idx = device % columns
        send_list = send_rows[:, col_idx, dom_idx, :]
        alive = send_list >= 0
        global_rows = ((owner_ids * columns + col_idx) * ent_dev)[:, None] + jnp.maximum(send_list, 0)
        incoming = jnp.where(alive[..., None], emb_table[global_rows], jnp.float32(0.0))
        incoming = incoming.reshape(owners * slot_cap, width)
        neg_global = ((dom_idx * columns + column_ids) * ent_dev)[:, None, None] + neg_rows[dom_idx]
        neg_global = jnp.transpose(neg_global, (1, 0, 2)).reshape(blocks, -1)
        negatives = emb_table[neg_global]
        source_idx = src_slot[dom_idx, col_idx]
        target_idx = dst_slot[dom_idx, col_idx]
        sources = incoming[source_idx].reshape(blocks, -1, width)
        targets = incoming[target_idx].reshape(blocks, -1, width)
        relation = rel_diag[block_rel[dom_idx, col_idx]][:, None, :]
        src_grad, dst_grad, neg_grad = block_grads(sources, targets, negatives, relation)
        slot_grads = jnp.zeros((owners * slot_cap, width), jnp.float32)
        slot_grads = slot_grads.at[source_idx].add(src_grad.reshape(-1, width))
        slot_grads = slot_grads.at[target_idx].add(dst_grad.reshape(-1, width))
        target_rows = jnp.where(alive, global_rows, ent_rows).reshape(-1)
        total_grad = total_grad.at[target_rows].add(slot_grads, mode="drop")
        total_grad = total_grad.at[neg_global.reshape(-1)].add(neg_grad.reshape(-1, width))
        return total_grad, None

    result, _ = lax.scan(device_step, jnp.zeros(emb_table.shape, jnp.float32),
                         jnp.arange(owners * columns, dtype=jnp.int32))
    return result
```

```python
import jax
import jax.numpy as jnp
from jax import lax
from jax.sharding import PartitionSpec as P


def block_grads(sources, targets, negatives, relation):
    highest = lax.Precision.HIGHEST
    query = sources * relation
    positive = jnp.sum(query * targets, axis=-1)
    scores = jnp.einsum("cek,cjk->cej", query, negatives, precision=highest)
    largest = jnp.maximum(jnp.max(scores, axis=-1), positive)
    pos_exp = jnp.exp(positive - largest)
    neg_exp = jnp.exp(scores - largest[..., None])
    total = pos_exp + jnp.sum(neg_exp, axis=-1)
    pos_weight = pos_exp / total - 1.0
    neg_weight = neg_exp / total[..., None]
    query_grad = pos_weight[..., None] * targets + jnp.einsum(
        "cej,cjk->cek", neg_weight, negatives, precision=highest
    )
    neg_grad = jnp.einsum("cej,cek->cjk", neg_weight, query, precision=highest)
    return (query_grad * relation, pos_weight[..., None] * query, neg_grad)


def on_device(emb_table, rel_diag, send_rows, src_slot, dst_slot, neg_rows, block_rel):
    ent_dev, width = emb_table.shape
    send_list = send_rows[0, 0]
    owners, slot_cap = send_list.shape
    alive = send_list >= 0
    picked = jnp.where(alive[..., None], emb_table[jnp.maximum(send_list, 0)], jnp.float32(0.0))
    incoming = lax.all_to_all(picked, "dom", split_axis=0, concat_axis=0, tiled=True).reshape(
        owners * slot_cap, width
    )
    blocks = block_rel.shape[2]
    source_idx = src_slot[0, 0]
    target_idx = dst_slot[0, 0]
    sources = incoming[source_idx].reshape(blocks, -1, width)
    targets = incoming[target_idx].reshape(blocks, -1, width)
    relation = rel_diag[block_rel[0, 0]][:, None, :]
    own_negs = emb_table[neg_rows[0, 0]]
    columns = lax.axis_size("bucket")
    neg_dev = own_negs.shape[1]
    sent = jnp.broadcast_to(own_negs[None], (columns, blocks, neg_dev, width))
    gathered = lax.all_to_all(sent, "bucket", split_axis=0, concat_axis=0, tiled=True)
    negatives = jnp.transpose(gathered, (1, 0, 2, 3)).reshape(blocks, columns * neg_dev, width)
    src_grad, dst_grad, neg_part = block_grads(sources, targets, negatives, relation)
    parts = jnp.transpose(neg_part.reshape(blocks, columns, neg_dev, width), (1, 0, 2, 3))
    returned = lax.all_to_all(parts, "bucket", split_axis=0, concat_axis=0, tiled=True)
    own_grad = jnp.sum(returned, axis=0)
    slot_grads = jnp.zeros((owners * slot_cap, width), jnp.float32)
    slot_grads = slot_grads.at[source_idx].add(src_grad.reshape(-1, width))
    slot_grads = slot_grads.at[target_idx].add(dst_grad.reshape(-1, width))
    returned_rows = lax.all_to_all(
        slot_grads.reshape(owners, slot_cap, width), "dom", split_axis=0, concat_axis=0, tiled=True
    )
    row_targets = jnp.where(alive, send_list, ent_dev).reshape(-1)
    result = jnp.zeros((ent_dev, width), jnp.float32)
    result = result.at[row_targets].add(returned_rows.reshape(-1, width), mode="drop")
    result = result.at[neg_rows[0, 0].reshape(-1)].add(own_grad.reshape(-1, width))
    return result


def solution(mesh):
    placed = (
        P(("dom", "bucket"), None),
        P(),
        P("dom", "bucket", None, None),
        P("dom", "bucket", None),
        P("dom", "bucket", None),
        P("dom", "bucket", None, None),
        P("dom", "bucket", None),
    )
    return jax.shard_map(
        on_device, mesh=mesh, in_specs=placed, out_specs=P(("dom", "bucket"), None), check_vma=False
    )
```

```python
import functools

import jax
import jax.numpy as jnp
from jax import lax
from jax.experimental import pallas as pl
from jax.experimental.pallas import tpu as pltpu
from jax.sharding import PartitionSpec as P

LANES = 128
CHUNKS = 4
TAIL = 16
WIDE = CHUNKS * LANES
HIGHEST = lax.Precision.HIGHEST
VMEM = pl.BlockSpec(memory_space=pltpu.VMEM)
SMEM = pl.BlockSpec(memory_space=pltpu.SMEM)


def split(x, terms):
    parts = []
    for _ in range(terms):
        part = x.astype(jnp.bfloat16)
        parts.append(part)
        x = x - part.astype(jnp.float32)
    return parts


def select_rows(onehot, x, terms):
    total = None
    for part in split(x, terms):
        product = jnp.dot(onehot, part, preferred_element_type=jnp.float32)
        total = product if total is None else total + product
    return total


def onehot_of(index, shape, axis):
    return jnp.where(index == lax.broadcasted_iota(jnp.int32, shape, axis), 1.0, 0.0).astype(jnp.bfloat16)


def pack(x, out_ref):
    owners = out_ref.shape[0]
    slots = x.shape[0] // owners
    group = slots // 4
    for j in range(CHUNKS - 1):
        out_ref[:, j * slots : (j + 1) * slots, :] = x[:, j * LANES : (j + 1) * LANES].reshape(owners, slots, LANES)
    tails = x[:, (CHUNKS - 1) * LANES :].reshape(owners, 4, group, LANES)
    tail = tails[:, 0].reshape(owners * group, LANES)
    for q in range(1, 4):
        tail = tail + pltpu.roll(tails[:, q].reshape(owners * group, LANES), TAIL * q, 1)
    out_ref[:, (CHUNKS - 1) * slots :, :] = tail.reshape(owners, group, LANES)


def unpack(ref, out_ref):
    owners = ref.shape[0]
    slots = out_ref.shape[0] // owners
    group = slots // 4
    for j in range(CHUNKS - 1):
        out_ref[:, j * LANES : (j + 1) * LANES] = ref[:, j * slots : (j + 1) * slots, :].reshape(owners * slots, LANES)
    tail = ref[:, (CHUNKS - 1) * slots :, :].reshape(owners * group, LANES)
    live = lax.broadcasted_iota(jnp.int32, tail.shape, 1) < TAIL
    tails = []
    for q in range(4):
        turned = tail if q == 0 else pltpu.roll(tail, LANES - TAIL * q, 1)
        tails.append(jnp.where(live, turned, 0.0).reshape(owners, group, LANES))
    out_ref[:, (CHUNKS - 1) * LANES :] = jnp.stack(tails, axis=1).reshape(owners * slots, LANES)


def widen(ref, out_ref):
    out_ref[:, WIDE - LANES :] = jnp.zeros((out_ref.shape[0], LANES), jnp.float32)
    out_ref[:, : ref.shape[1]] = ref[...]


def pick_kernel(neg_ref, send_ref, table_ref, rows_ref, negs_ref, table):
    widen(table_ref, table)
    for n in range(neg_ref.shape[0]):
        row = table[pl.ds(neg_ref[n], 1), :]
        for j in range(CHUNKS):
            negs_ref[j * 4 + n : j * 4 + n + 1, :] = row[:, j * LANES : (j + 1) * LANES]
    slots, entities = send_ref.shape[0], table_ref.shape[0]
    onehot = onehot_of(send_ref[...], (slots, entities), 1)
    pack(select_rows(onehot, table[...], 3), rows_ref)


def grad_kernel(col_ref, row_ref, rel_ref, got_ref, negs_ref, back_ref, negs_back_ref, rows, negs, grads):
    unpack(got_ref, rows)
    slots, ends = rows.shape[0], col_ref.shape[0]
    edges = ends // 2
    blocks = rel_ref.shape[0]
    block = edges // blocks
    owners = negs_ref.shape[0] // 16
    picked = select_rows(onehot_of(col_ref[...], (ends, slots), 1), rows[...], 3)
    for c in range(blocks):
        for k in range(2):
            for j in range(CHUNKS):
                negs[k * owners : (k + 1) * owners, j * LANES : (j + 1) * LANES] = negs_ref[
                    pl.ds(j * 4 + c * 2 + k, owners, stride=16), :
                ]
        negatives = negs[...]
        relation = rel_ref[c : c + 1, :]
        query = picked[c * block : (c + 1) * block] * relation
        target = picked[edges + c * block : edges + (c + 1) * block]
        positive = jnp.sum(query * target, axis=1, keepdims=True)
        scores = lax.dot_general(
            query, negatives, (((1,), (1,)), ((), ())), precision=HIGHEST, preferred_element_type=jnp.float32
        )
        largest = jnp.maximum(jnp.max(scores, axis=1, keepdims=True), positive)
        pos_exp = jnp.exp(positive - largest)
        neg_exp = jnp.exp(scores - largest)
        total = pos_exp + jnp.sum(neg_exp, axis=1, keepdims=True)
        pos_weight = pos_exp / total - 1.0
        weight = neg_exp / total
        query_grad = pos_weight * target + jnp.dot(
            weight, negatives, precision=HIGHEST, preferred_element_type=jnp.float32
        )
        grads[c * block : (c + 1) * block, :] = query_grad * relation
        grads[edges + c * block : edges + (c + 1) * block, :] = pos_weight * query
        neg_grad = jnp.dot(weight.T, query, precision=HIGHEST, preferred_element_type=jnp.float32)
        for k in range(2):
            for j in range(CHUNKS):
                negs_back_ref[pl.ds(j * 4 + c * 2 + k, owners, stride=16), :] = neg_grad[
                    k * owners : (k + 1) * owners, j * LANES : (j + 1) * LANES
                ]
    pack(select_rows(onehot_of(row_ref[...], (slots, ends), 0), grads[...], 2), back_ref)


def put_kernel(neg_ref, send_ref, got_ref, negs_ref, out_ref, rows):
    unpack(got_ref, rows)
    entities, width = out_ref.shape
    result = select_rows(onehot_of(send_ref[...], (entities, rows.shape[0]), 0), rows[...], 2)
    own = jnp.sum(negs_ref[...], axis=0)
    place = lax.broadcasted_iota(jnp.int32, (entities, LANES), 0)
    for j in range(CHUNKS):
        part = result[:, j * LANES : (j + 1) * LANES]
        for n in range(neg_ref.shape[0]):
            part = part + jnp.where(place == neg_ref[n], own[j * 4 + n : j * 4 + n + 1, :], 0.0)
        stop = min(width, (j + 1) * LANES)
        out_ref[:, j * LANES : stop] = part[:, : stop - j * LANES]


def shaped(*shape):
    return jax.ShapeDtypeStruct(shape, jnp.float32)


def scratch(*shape):
    return pltpu.VMEM(shape, jnp.float32)


def on_device(emb_table, rel_diag, send_rows, src_slot, dst_slot, neg_rows, block_rel):
    entities, width = emb_table.shape
    owners, slots = send_rows.shape[2:]
    columns = lax.axis_size("bucket")
    packed = (owners, (CHUNKS - 1) * slots + slots // 4, LANES)
    send = send_rows.reshape(owners * slots)
    own_rows = neg_rows.reshape(4)
    picked, own_negs = pl.pallas_call(
        pick_kernel,
        out_shape=(shaped(*packed), shaped(16, LANES)),
        in_specs=[SMEM, VMEM, VMEM],
        out_specs=(VMEM, VMEM),
        scratch_shapes=[scratch(entities, WIDE)],
        name="pick",
    )(own_rows, send[:, None], emb_table)
    negs = lax.all_to_all(
        jnp.broadcast_to(own_negs, (columns, 16, LANES)), "bucket", split_axis=0, concat_axis=0, tiled=True
    )
    got = lax.all_to_all(picked, "dom", split_axis=0, concat_axis=0, tiled=True)
    ends = jnp.concatenate([src_slot.reshape(-1), dst_slot.reshape(-1)])
    relation = jnp.pad(rel_diag[block_rel.reshape(-1)], ((0, 0), (0, WIDE - width)))
    back, negs_back = pl.pallas_call(
        grad_kernel,
        out_shape=(shaped(*packed), shaped(columns * 16, LANES)),
        in_specs=[VMEM] * 5,
        out_specs=(VMEM, VMEM),
        scratch_shapes=[
            scratch(owners * slots, WIDE),
            scratch(2 * columns, WIDE),
            scratch(ends.shape[0], WIDE),
        ],
        name="grad",
    )(ends[:, None], ends[None, :], relation, got, negs.reshape(columns * 16, LANES))
    own_grad = lax.all_to_all(
        negs_back.reshape(columns, 16, LANES), "bucket", split_axis=0, concat_axis=0, tiled=True
    )
    returned = lax.all_to_all(back, "dom", split_axis=0, concat_axis=0, tiled=True)
    return pl.pallas_call(
        put_kernel,
        out_shape=shaped(entities, width),
        in_specs=[SMEM, VMEM, VMEM, VMEM],
        out_specs=VMEM,
        scratch_shapes=[scratch(owners * slots, WIDE)],
        name="put",
    )(own_rows, send[None, :], returned, own_grad)


def solution(mesh):
    placed = (
        P(("dom", "bucket"), None),
        P(),
        P("dom", "bucket", None, None),
        P("dom", "bucket", None),
        P("dom", "bucket", None),
        P("dom", "bucket", None, None),
        P("dom", "bucket", None),
    )
    return jax.shard_map(
        on_device, mesh=mesh, in_specs=placed, out_specs=P(("dom", "bucket"), None), check_vma=False
    )
```

```python
import functools

import jax
import jax.numpy as jnp
from jax import lax
from jax.experimental import pallas as pl
from jax.experimental.pallas import tpu as pltpu
from jax.sharding import PartitionSpec as P

LANES = 128
CHUNKS = 4
TAIL = 16
WIDE = CHUNKS * LANES
HIGHEST = lax.Precision.HIGHEST
VMEM = pl.BlockSpec(memory_space=pltpu.VMEM)
SMEM = pl.BlockSpec(memory_space=pltpu.SMEM)


def split(x, terms):
    parts = []
    for _ in range(terms):
        part = x.astype(jnp.bfloat16)
        parts.append(part)
        x = x - part.astype(jnp.float32)
    return parts


def select_rows(onehot, x, terms):
    total = None
    for part in split(x, terms):
        product = jnp.dot(onehot, part, preferred_element_type=jnp.float32)
        total = product if total is None else total + product
    return total


def onehot_of(index, shape, axis):
    return jnp.where(index == lax.broadcasted_iota(jnp.int32, shape, axis), 1.0, 0.0).astype(jnp.bfloat16)


def pack(x, out_ref):
    owners = out_ref.shape[0]
    slots = x.shape[0] // owners
    group = slots // 4
    for j in range(CHUNKS - 1):
        out_ref[:, j * slots : (j + 1) * slots, :] = x[:, j * LANES : (j + 1) * LANES].reshape(owners, slots, LANES)
    tails = x[:, (CHUNKS - 1) * LANES :].reshape(owners, 4, group, LANES)
    tail = tails[:, 0].reshape(owners * group, LANES)
    for q in range(1, 4):
        tail = tail + pltpu.roll(tails[:, q].reshape(owners * group, LANES), TAIL * q, 1)
    out_ref[:, (CHUNKS - 1) * slots :, :] = tail.reshape(owners, group, LANES)


def unpack(ref, out_ref):
    owners = ref.shape[0]
    slots = out_ref.shape[0] // owners
    group = slots // 4
    for j in range(CHUNKS - 1):
        out_ref[:, j * LANES : (j + 1) * LANES] = ref[:, j * slots : (j + 1) * slots, :].reshape(owners * slots, LANES)
    tail = ref[:, (CHUNKS - 1) * slots :, :].reshape(owners * group, LANES)
    live = lax.broadcasted_iota(jnp.int32, tail.shape, 1) < TAIL
    tails = []
    for q in range(4):
        turned = tail if q == 0 else pltpu.roll(tail, LANES - TAIL * q, 1)
        tails.append(jnp.where(live, turned, 0.0).reshape(owners, group, LANES))
    out_ref[:, (CHUNKS - 1) * LANES :] = jnp.stack(tails, axis=1).reshape(owners * slots, LANES)


def widen(ref, out_ref):
    out_ref[:, WIDE - LANES :] = jnp.zeros((out_ref.shape[0], LANES), jnp.float32)
    out_ref[:, : ref.shape[1]] = ref[...]


def pick_kernel(neg_ref, send_ref, table_ref, rows_ref, negs_ref, table):
    widen(table_ref, table)
    for n in range(neg_ref.shape[0]):
        row = table[pl.ds(neg_ref[n], 1), :]
        for j in range(CHUNKS):
            negs_ref[j * 4 + n : j * 4 + n + 1, :] = row[:, j * LANES : (j + 1) * LANES]
    slots, entities = send_ref.shape[0], table_ref.shape[0]
    onehot = onehot_of(send_ref[...], (slots, entities), 1)
    pack(select_rows(onehot, table[...], 3), rows_ref)


def grad_kernel(col_ref, row_ref, rel_ref, got_ref, negs_ref, back_ref, negs_back_ref, rows, negs, grads):
    unpack(got_ref, rows)
    slots, ends = rows.shape[0], col_ref.shape[0]
    edges = ends // 2
    blocks = rel_ref.shape[0]
    block = edges // blocks
    owners = negs_ref.shape[0] // 16
    picked = select_rows(onehot_of(col_ref[...], (ends, slots), 1), rows[...], 3)
    for c in range(blocks):
        for k in range(2):
            for j in range(CHUNKS):
                negs[k * owners : (k + 1) * owners, j * LANES : (j + 1) * LANES] = negs_ref[
                    pl.ds(j * 4 + c * 2 + k, owners, stride=16), :
                ]
        negatives = negs[...]
        relation = rel_ref[c : c + 1, :]
        query = picked[c * block : (c + 1) * block] * relation
        target = picked[edges + c * block : edges + (c + 1) * block]
        positive = jnp.sum(query * target, axis=1, keepdims=True)
        scores = lax.dot_general(
            query, negatives, (((1,), (1,)), ((), ())), precision=HIGHEST, preferred_element_type=jnp.float32
        )
        largest = jnp.maximum(jnp.max(scores, axis=1, keepdims=True), positive)
        pos_exp = jnp.exp(positive - largest)
        neg_exp = jnp.exp(scores - largest)
        total = pos_exp + jnp.sum(neg_exp, axis=1, keepdims=True)
        pos_weight = pos_exp / total - 1.0
        weight = neg_exp / total
        query_grad = pos_weight * target + jnp.dot(
            weight, negatives, precision=HIGHEST, preferred_element_type=jnp.float32
        )
        grads[c * block : (c + 1) * block, :] = query_grad * relation
        grads[edges + c * block : edges + (c + 1) * block, :] = pos_weight * query
        neg_grad = jnp.dot(weight.T, query, precision=HIGHEST, preferred_element_type=jnp.float32)
        for k in range(2):
            for j in range(CHUNKS):
                negs_back_ref[pl.ds(j * 4 + c * 2 + k, owners, stride=16), :] = neg_grad[
                    k * owners : (k + 1) * owners, j * LANES : (j + 1) * LANES
                ]
    pack(select_rows(onehot_of(row_ref[...], (slots, ends), 0), grads[...], 2), back_ref)


def put_kernel(neg_ref, send_ref, got_ref, negs_ref, out_ref, rows):
    unpack(got_ref, rows)
    entities, width = out_ref.shape
    result = select_rows(onehot_of(send_ref[...], (entities, rows.shape[0]), 0), rows[...], 2)
    own = negs_ref[...]
    place = lax.broadcasted_iota(jnp.int32, (entities, LANES), 0)
    for j in range(CHUNKS):
        part = result[:, j * LANES : (j + 1) * LANES]
        for n in range(neg_ref.shape[0]):
            part = part + jnp.where(place == neg_ref[n], own[j * 4 + n : j * 4 + n + 1, :], 0.0)
        stop = min(width, (j + 1) * LANES)
        out_ref[:, j * LANES : stop] = part[:, : stop - j * LANES]


def shaped(*shape):
    return jax.ShapeDtypeStruct(shape, jnp.float32)


def scratch(*shape):
    return pltpu.VMEM(shape, jnp.float32)


def digits(columns):
    side = 1
    while side * side < columns:
        side *= 2
    def both(b, s):
        return b ^ ((s & 1) | ((s >> 1) * side))

    def along_z(b, s):
        y, z = divmod(b, side)
        return y * side + (z + 2 * s) % side

    def along_y(b, s):
        y, z = divmod(b, side)
        return ((y + 2 * s) % (columns // side)) * side + z

    return along_z, along_y, both


def fetch(x, turn, step, columns):
    return lax.ppermute(x, "bucket", [(turn(b, step), b) for b in range(columns)])


def hand(x, turn, step, columns):
    return lax.ppermute(x, "bucket", [(b, turn(b, step)) for b in range(columns)])


def gather_columns(x, columns):
    for turn in digits(columns):
        x = jnp.stack([x] + [fetch(x, turn, step, columns) for step in range(1, 4)])
    return x


def sum_columns(x, columns):
    for turn in reversed(digits(columns)):
        x = x[0] + sum(hand(x[step], turn, step, columns) for step in range(1, 4))
    return x


def on_device(emb_table, rel_diag, send_rows, src_slot, dst_slot, neg_rows, block_rel):
    entities, width = emb_table.shape
    owners, slots = send_rows.shape[2:]
    columns = lax.axis_size("bucket")
    packed = (owners, (CHUNKS - 1) * slots + slots // 4, LANES)
    send = send_rows.reshape(owners * slots)
    own_rows = neg_rows.reshape(4)
    picked, own_negs = pl.pallas_call(
        pick_kernel,
        out_shape=(shaped(*packed), shaped(16, LANES)),
        in_specs=[SMEM, VMEM, VMEM],
        out_specs=(VMEM, VMEM),
        scratch_shapes=[scratch(entities, WIDE)],
        name="pick",
    )(own_rows, send[:, None], emb_table)
    negs = gather_columns(own_negs, columns)
    got = lax.all_to_all(picked, "dom", split_axis=0, concat_axis=0, tiled=True)
    ends = jnp.concatenate([src_slot.reshape(-1), dst_slot.reshape(-1)])
    relation = jnp.pad(rel_diag[block_rel.reshape(-1)], ((0, 0), (0, WIDE - width)))
    back, negs_back = pl.pallas_call(
        grad_kernel,
        out_shape=(shaped(*packed), shaped(columns * 16, LANES)),
        in_specs=[VMEM] * 5,
        out_specs=(VMEM, VMEM),
        scratch_shapes=[
            scratch(owners * slots, WIDE),
            scratch(2 * columns, WIDE),
            scratch(ends.shape[0], WIDE),
        ],
        name="grad",
    )(ends[:, None], ends[None, :], relation, got, negs.reshape(columns * 16, LANES))
    own_grad = sum_columns(negs_back.reshape(4, 4, 4, 16, LANES), columns)
    returned = lax.all_to_all(back, "dom", split_axis=0, concat_axis=0, tiled=True)
    return pl.pallas_call(
        put_kernel,
        out_shape=shaped(entities, width),
        in_specs=[SMEM, VMEM, VMEM, VMEM],
        out_specs=VMEM,
        scratch_shapes=[scratch(owners * slots, WIDE)],
        name="put",
    )(own_rows, send[None, :], returned, own_grad)


def solution(mesh):
    placed = (
        P(("dom", "bucket"), None),
        P(),
        P("dom", "bucket", None, None),
        P("dom", "bucket", None),
        P("dom", "bucket", None),
        P("dom", "bucket", None, None),
        P("dom", "bucket", None),
    )
    return jax.shard_map(
        on_device, mesh=mesh, in_specs=placed, out_specs=P(("dom", "bucket"), None), check_vma=False
    )
```

```python
import functools

import jax
import jax.numpy as jnp
from jax import lax
from jax.experimental import pallas as pl
from jax.experimental.pallas import tpu as pltpu
from jax.sharding import PartitionSpec as P

LANES = 128
CHUNKS = 4
TAIL = 16
WIDE = CHUNKS * LANES
HIGHEST = lax.Precision.HIGHEST
VMEM = pl.BlockSpec(memory_space=pltpu.VMEM)


def split(x, terms):
    parts = []
    for _ in range(terms):
        part = x.astype(jnp.bfloat16)
        parts.append(part)
        x = x - part.astype(jnp.float32)
    return parts


def select_rows(onehot, x, terms):
    total = None
    for part in split(x, terms):
        product = jnp.dot(onehot, part, preferred_element_type=jnp.float32)
        total = product if total is None else total + product
    return total


def onehot_of(index, shape, axis):
    return jnp.where(index == lax.broadcasted_iota(jnp.int32, shape, axis), 1.0, 0.0).astype(jnp.bfloat16)


def pack(x, out_ref):
    owners = out_ref.shape[0]
    slots = x.shape[0] // owners
    group = slots // 4
    for j in range(CHUNKS - 1):
        out_ref[:, j * slots : (j + 1) * slots, :] = x[:, j * LANES : (j + 1) * LANES].reshape(owners, slots, LANES)
    tails = x[:, (CHUNKS - 1) * LANES :].reshape(owners, 4, group, LANES)
    tail = tails[:, 0].reshape(owners * group, LANES)
    for q in range(1, 4):
        tail = tail + pltpu.roll(tails[:, q].reshape(owners * group, LANES), TAIL * q, 1)
    out_ref[:, (CHUNKS - 1) * slots :, :] = tail.reshape(owners, group, LANES)


def unpack(ref, out_ref):
    owners = ref.shape[0]
    slots = out_ref.shape[0] // owners
    group = slots // 4
    for j in range(CHUNKS - 1):
        out_ref[:, j * LANES : (j + 1) * LANES] = ref[:, j * slots : (j + 1) * slots, :].reshape(owners * slots, LANES)
    tail = ref[:, (CHUNKS - 1) * slots :, :].reshape(owners * group, LANES)
    live = lax.broadcasted_iota(jnp.int32, tail.shape, 1) < TAIL
    tails = []
    for q in range(4):
        turned = tail if q == 0 else pltpu.roll(tail, LANES - TAIL * q, 1)
        tails.append(jnp.where(live, turned, 0.0).reshape(owners, group, LANES))
    out_ref[:, (CHUNKS - 1) * LANES :] = jnp.stack(tails, axis=1).reshape(owners * slots, LANES)


def widen(ref, out_ref):
    width = ref.shape[0]
    out_ref[:width, :] = ref[...]
    out_ref[width:, :] = jnp.zeros((out_ref.shape[0] - width, out_ref.shape[1]), jnp.float32)


def select_columns(onehot, x, terms):
    total = None
    for part in split(x, terms):
        product = lax.dot_general(onehot, part, (((1,), (1,)), ((), ())), preferred_element_type=jnp.float32)
        total = product if total is None else total + product
    return total


def own_row(neg_ref, n):
    return neg_ref[0, 0, n // 2 : n // 2 + 1, n % 2 : n % 2 + 1]


def negs_kernel(neg_ref, table_ref, out_ref, table):
    widen(table_ref, table)
    entities = table.shape[1]
    place = lax.broadcasted_iota(jnp.int32, (8, entities), 0)
    entity = lax.broadcasted_iota(jnp.int32, (8, entities), 1)
    hit = jnp.zeros((8, entities), jnp.float32)
    for n in range(4):
        hit = jnp.where((place == n) & (entity == own_row(neg_ref, n)), 1.0, hit)
    rows = select_columns(hit.astype(jnp.bfloat16), table[...], 3)
    for j in range(CHUNKS):
        out_ref[j * 4 : j * 4 + 4, :] = rows[:4, j * LANES : (j + 1) * LANES]


def pick_kernel(send_ref, table_ref, rows_ref, table):
    widen(table_ref, table)
    onehot = onehot_of(send_ref[...], (send_ref.shape[0], table.shape[1]), 1)
    pack(select_columns(onehot, table[...], 3), rows_ref)


def grad_kernel(col_ref, row_ref, rel_ref, got_ref, negs_ref, back_ref, negs_back_ref, rows, negs, grads):
    unpack(got_ref, rows)
    slots, ends = rows.shape[0], col_ref.shape[0]
    edges = ends // 2
    blocks = rel_ref.shape[0]
    block = edges // blocks
    owners = negs_ref.shape[0] // 16
    picked = select_rows(onehot_of(col_ref[...], (ends, slots), 1), rows[...], 3)
    for c in range(blocks):
        for k in range(2):
            for j in range(CHUNKS):
                negs[k * owners : (k + 1) * owners, j * LANES : (j + 1) * LANES] = negs_ref[
                    pl.ds(j * 4 + c * 2 + k, owners, stride=16), :
                ]
        negatives = negs[...]
        relation = rel_ref[c : c + 1, :]
        query = picked[c * block : (c + 1) * block] * relation
        target = picked[edges + c * block : edges + (c + 1) * block]
        positive = jnp.sum(query * target, axis=1, keepdims=True)
        scores = lax.dot_general(
            query, negatives, (((1,), (1,)), ((), ())), precision=HIGHEST, preferred_element_type=jnp.float32
        )
        largest = jnp.maximum(jnp.max(scores, axis=1, keepdims=True), positive)
        pos_exp = jnp.exp(positive - largest)
        neg_exp = jnp.exp(scores - largest)
        total = pos_exp + jnp.sum(neg_exp, axis=1, keepdims=True)
        pos_weight = pos_exp / total - 1.0
        weight = neg_exp / total
        query_grad = pos_weight * target + jnp.dot(
            weight, negatives, precision=HIGHEST, preferred_element_type=jnp.float32
        )
        grads[c * block : (c + 1) * block, :] = query_grad * relation
        grads[edges + c * block : edges + (c + 1) * block, :] = pos_weight * query
        neg_grad = jnp.dot(weight.T, query, precision=HIGHEST, preferred_element_type=jnp.float32)
        for k in range(2):
            for j in range(CHUNKS):
                negs_back_ref[pl.ds(j * 4 + c * 2 + k, owners, stride=16), :] = neg_grad[
                    k * owners : (k + 1) * owners, j * LANES : (j + 1) * LANES
                ]
    pack(select_rows(onehot_of(row_ref[...], (slots, ends), 0), grads[...], 2), back_ref)


def put_kernel(send_ref, got_ref, out_ref, rows):
    unpack(got_ref, rows)
    entities = out_ref.shape[1]
    out_ref[...] = select_rows(onehot_of(send_ref[...], (entities, rows.shape[0]), 0), rows[...], 2).T


def add_kernel(neg_ref, put_ref, parts_ref, out_ref):
    own = jnp.sum(parts_ref[...], axis=0).T
    width, entities = out_ref.shape
    for j in range(CHUNKS):
        stop = min(width, (j + 1) * LANES) - j * LANES
        part = put_ref[j * LANES : j * LANES + stop, :]
        entity = lax.broadcasted_iota(jnp.int32, part.shape, 1)
        for n in range(4):
            part = part + jnp.where(entity == own_row(neg_ref, n), own[:stop, j * 4 + n : j * 4 + n + 1], 0.0)
        out_ref[j * LANES : j * LANES + stop, :] = part


def shaped(*shape):
    return jax.ShapeDtypeStruct(shape, jnp.float32)


def scratch(*shape):
    return pltpu.VMEM(shape, jnp.float32)


def even_groups(columns):
    side = 1
    while side * side < columns:
        side *= 2
    groups = []
    for low_y in range(2):
        for low_z in range(2):
            ys, zs = range(low_y, columns // side, 2), range(low_z, side, 2)
            groups.append([y * side + z for y in ys for z in zs])
    return side, groups


def swap(x, bit, columns):
    return lax.ppermute(x, "bucket", [(b, b ^ bit) for b in range(columns)])


def gather_columns(x, columns):
    side, groups = even_groups(columns)
    x = jnp.broadcast_to(x, (len(groups[0]), *x.shape))
    x = lax.all_to_all(x, "bucket", split_axis=0, concat_axis=0, axis_index_groups=groups, tiled=True)
    for bit in (1, side):
        x = jnp.stack([x, swap(x, bit, columns)])
    return x


def sum_columns(x, columns):
    side, groups = even_groups(columns)
    x = x.reshape(2, 2, len(groups[0]), 16, LANES)
    for bit in (side, 1):
        x = x[0] + swap(x[1], bit, columns)
    return lax.all_to_all(x, "bucket", split_axis=0, concat_axis=0, axis_index_groups=groups, tiled=True)


def on_device(emb_table, rel_diag, send_rows, src_slot, dst_slot, neg_rows, block_rel):
    entities, width = emb_table.shape
    owners, slots = send_rows.shape[2:]
    columns = lax.axis_size("bucket")
    packed = (owners, (CHUNKS - 1) * slots + slots // 4, LANES)
    send = send_rows.reshape(owners * slots)
    table = emb_table.T
    own_negs = pl.pallas_call(
        negs_kernel,
        out_shape=shaped(16, LANES),
        in_specs=[VMEM, VMEM],
        out_specs=VMEM,
        scratch_shapes=[scratch(WIDE, entities)],
        name="negs",
    )(neg_rows, table)
    picked = pl.pallas_call(
        pick_kernel,
        out_shape=shaped(*packed),
        in_specs=[VMEM, VMEM],
        out_specs=VMEM,
        scratch_shapes=[scratch(WIDE, entities)],
        name="pick",
    )(send[:, None], table)
    negs = gather_columns(own_negs, columns)
    got = lax.all_to_all(picked, "dom", split_axis=0, concat_axis=0, tiled=True)
    ends = jnp.concatenate([src_slot.reshape(-1), dst_slot.reshape(-1)])
    relation = jnp.pad(rel_diag[block_rel.reshape(-1)], ((0, 0), (0, WIDE - width)))
    back, negs_back = pl.pallas_call(
        grad_kernel,
        out_shape=(shaped(*packed), shaped(columns * 16, LANES)),
        in_specs=[VMEM] * 5,
        out_specs=(VMEM, VMEM),
        scratch_shapes=[
            scratch(owners * slots, WIDE),
            scratch(2 * columns, WIDE),
            scratch(ends.shape[0], WIDE),
        ],
        name="grad",
    )(ends[:, None], ends[None, :], relation, got, negs.reshape(columns * 16, LANES))
    own_grad = sum_columns(negs_back, columns)
    returned = lax.all_to_all(back, "dom", split_axis=0, concat_axis=0, tiled=True)
    put = pl.pallas_call(
        put_kernel,
        out_shape=shaped(WIDE, entities),
        in_specs=[VMEM, VMEM],
        out_specs=VMEM,
        scratch_shapes=[scratch(owners * slots, WIDE)],
        name="put",
    )(send[None, :], returned)
    return pl.pallas_call(
        add_kernel,
        out_shape=shaped(width, entities),
        in_specs=[VMEM, VMEM, VMEM],
        out_specs=VMEM,
        name="add",
    )(neg_rows, put, own_grad).T


def solution(mesh):
    placed = (
        P(("dom", "bucket"), None),
        P(),
        P("dom", "bucket", None, None),
        P("dom", "bucket", None),
        P("dom", "bucket", None),
        P("dom", "bucket", None, None),
        P("dom", "bucket", None),
    )
    return jax.shard_map(
        on_device, mesh=mesh, in_specs=placed, out_specs=P(("dom", "bucket"), None), check_vma=False
    )
```

```python
import functools

import jax
import jax.numpy as jnp
from jax import lax
from jax.experimental import pallas as pl
from jax.experimental.pallas import tpu as pltpu
from jax.sharding import PartitionSpec as P

LANES = 128
CHUNKS = 4
TAIL = 16
WIDE = CHUNKS * LANES
HIGHEST = lax.Precision.HIGHEST
VMEM = pl.BlockSpec(memory_space=pltpu.VMEM)


def split(x, terms):
    parts = []
    for _ in range(terms):
        part = x.astype(jnp.bfloat16)
        parts.append(part)
        x = x - part.astype(jnp.float32)
    return parts


def select_rows(onehot, x, terms):
    total = None
    for part in split(x, terms):
        product = jnp.dot(onehot, part, preferred_element_type=jnp.float32)
        total = product if total is None else total + product
    return total


def onehot_of(index, shape, axis):
    return jnp.where(index == lax.broadcasted_iota(jnp.int32, shape, axis), 1.0, 0.0).astype(jnp.bfloat16)


def pack(x, out_ref):
    owners = out_ref.shape[0]
    slots = x.shape[0] // owners
    group = slots // 4
    for j in range(CHUNKS - 1):
        out_ref[:, j * slots : (j + 1) * slots, :] = x[:, j * LANES : (j + 1) * LANES].reshape(owners, slots, LANES)
    tails = x[:, (CHUNKS - 1) * LANES :].reshape(owners, 4, group, LANES)
    tail = tails[:, 0].reshape(owners * group, LANES)
    for q in range(1, 4):
        tail = tail + pltpu.roll(tails[:, q].reshape(owners * group, LANES), TAIL * q, 1)
    out_ref[:, (CHUNKS - 1) * slots :, :] = tail.reshape(owners, group, LANES)


def unpack(ref, out_ref):
    owners = ref.shape[0]
    slots = out_ref.shape[0] // owners
    group = slots // 4
    for j in range(CHUNKS - 1):
        out_ref[:, j * LANES : (j + 1) * LANES] = ref[:, j * slots : (j + 1) * slots, :].reshape(owners * slots, LANES)
    tail = ref[:, (CHUNKS - 1) * slots :, :].reshape(owners * group, LANES)
    live = lax.broadcasted_iota(jnp.int32, tail.shape, 1) < TAIL
    tails = []
    for q in range(4):
        turned = tail if q == 0 else pltpu.roll(tail, LANES - TAIL * q, 1)
        tails.append(jnp.where(live, turned, 0.0).reshape(owners, group, LANES))
    out_ref[:, (CHUNKS - 1) * LANES :] = jnp.stack(tails, axis=1).reshape(owners * slots, LANES)


def widen(ref, out_ref):
    width = ref.shape[0]
    out_ref[:width, :] = ref[...]
    out_ref[width:, :] = jnp.zeros((out_ref.shape[0] - width, out_ref.shape[1]), jnp.float32)


def select_columns(onehot, x, terms):
    total = None
    for part in split(x, terms):
        product = lax.dot_general(onehot, part, (((1,), (1,)), ((), ())), preferred_element_type=jnp.float32)
        total = product if total is None else total + product
    return total


def own_row(neg_ref, n):
    return neg_ref[0, 0, n // 2 : n // 2 + 1, n % 2 : n % 2 + 1]


def negs_kernel(neg_ref, table_ref, out_ref, table):
    widen(table_ref, table)
    entities = table.shape[1]
    place = lax.broadcasted_iota(jnp.int32, (8, entities), 0)
    entity = lax.broadcasted_iota(jnp.int32, (8, entities), 1)
    hit = jnp.zeros((8, entities), jnp.float32)
    for n in range(4):
        hit = jnp.where((place == n) & (entity == own_row(neg_ref, n)), 1.0, hit)
    rows = select_columns(hit.astype(jnp.bfloat16), table[...], 3)
    for j in range(CHUNKS):
        part = rows[:4, j * LANES : (j + 1) * LANES]
        out_ref[:, j * 4 : j * 4 + 4, :] = jnp.broadcast_to(part, (out_ref.shape[0], 4, LANES))


def pick_kernel(send_ref, table_ref, rows_ref, table):
    widen(table_ref, table)
    onehot = onehot_of(send_ref[...], (send_ref.shape[0], table.shape[1]), 1)
    pack(select_columns(onehot, table[...], 3), rows_ref)


def grad_kernel(col_ref, row_ref, rel_ref, got_ref, negs_ref, back_ref, negs_back_ref, rows, negs, grads):
    unpack(got_ref, rows)
    slots, ends = rows.shape[0], col_ref.shape[0]
    edges = ends // 2
    blocks = rel_ref.shape[0]
    block = edges // blocks
    owners = negs_ref.shape[0] // 16
    picked = select_rows(onehot_of(col_ref[...], (ends, slots), 1), rows[...], 3)
    for c in range(blocks):
        for k in range(2):
            for j in range(CHUNKS):
                negs[k * owners : (k + 1) * owners, j * LANES : (j + 1) * LANES] = negs_ref[
                    pl.ds(j * 4 + c * 2 + k, owners, stride=16), :
                ]
        negatives = negs[...]
        relation = rel_ref[c : c + 1, :]
        query = picked[c * block : (c + 1) * block] * relation
        target = picked[edges + c * block : edges + (c + 1) * block]
        positive = jnp.sum(query * target, axis=1, keepdims=True)
        scores = lax.dot_general(
            query, negatives, (((1,), (1,)), ((), ())), precision=HIGHEST, preferred_element_type=jnp.float32
        )
        largest = jnp.maximum(jnp.max(scores, axis=1, keepdims=True), positive)
        pos_exp = jnp.exp(positive - largest)
        neg_exp = jnp.exp(scores - largest)
        total = pos_exp + jnp.sum(neg_exp, axis=1, keepdims=True)
        pos_weight = pos_exp / total - 1.0
        weight = neg_exp / total
        query_grad = pos_weight * target + jnp.dot(
            weight, negatives, precision=HIGHEST, preferred_element_type=jnp.float32
        )
        grads[c * block : (c + 1) * block, :] = query_grad * relation
        grads[edges + c * block : edges + (c + 1) * block, :] = pos_weight * query
        neg_grad = jnp.dot(weight.T, query, precision=HIGHEST, preferred_element_type=jnp.float32)
        for k in range(2):
            for j in range(CHUNKS):
                negs_back_ref[pl.ds(j * 4 + c * 2 + k, owners, stride=16), :] = neg_grad[
                    k * owners : (k + 1) * owners, j * LANES : (j + 1) * LANES
                ]
    pack(select_rows(onehot_of(row_ref[...], (slots, ends), 0), grads[...], 2), back_ref)


def put_kernel(send_ref, got_ref, out_ref, rows):
    unpack(got_ref, rows)
    entities = out_ref.shape[1]
    out_ref[...] = select_rows(onehot_of(send_ref[...], (entities, rows.shape[0]), 0), rows[...], 2).T


def add_kernel(neg_ref, put_ref, parts_ref, out_ref):
    own = jnp.sum(parts_ref[...], axis=0).T
    width, entities = out_ref.shape
    for j in range(CHUNKS):
        stop = min(width, (j + 1) * LANES) - j * LANES
        part = put_ref[j * LANES : j * LANES + stop, :]
        entity = lax.broadcasted_iota(jnp.int32, part.shape, 1)
        for n in range(4):
            part = part + jnp.where(entity == own_row(neg_ref, n), own[:stop, j * 4 + n : j * 4 + n + 1], 0.0)
        out_ref[j * LANES : j * LANES + stop, :] = part


def near(x):
    return pltpu.with_memory_space_constraint(x, pltpu.VMEM)


def shaped(*shape):
    return jax.ShapeDtypeStruct(shape, jnp.float32)


def in_vmem(*shape):
    return pltpu.VMEM(shape, jnp.float32)


def quarters(columns):
    side = 1
    while side * side < columns:
        side *= 2
    depth = columns // side
    groups = [
        [y * side + z for y in range(top, top + depth // 2) for z in range(left, left + side // 2)]
        for top in (0, depth // 2)
        for left in (0, side // 2)
    ]

    def mirror(flip_y, flip_z):
        pairs = []
        for b in range(columns):
            y, z = divmod(b, side)
            pairs.append((b, (depth - 1 - y if flip_y else y) * side + (side - 1 - z if flip_z else z)))
        return pairs

    return groups, [mirror(False, True), mirror(True, False), mirror(True, True)]


def gather_columns(x, columns):
    groups, mirrors = quarters(columns)
    x = lax.all_to_all(x, "bucket", split_axis=0, concat_axis=0, axis_index_groups=groups, tiled=True)
    return jnp.stack([x] + [lax.ppermute(x, "bucket", pairs) for pairs in mirrors])


def sum_columns(x, columns):
    groups, mirrors = quarters(columns)
    x = x.reshape(4, len(groups[0]), 16, LANES)
    x = x[0] + sum(lax.ppermute(x[i + 1], "bucket", pairs) for i, pairs in enumerate(mirrors))
    return lax.all_to_all(x, "bucket", split_axis=0, concat_axis=0, axis_index_groups=groups, tiled=True)


def on_device(emb_table, rel_diag, send_rows, src_slot, dst_slot, neg_rows, block_rel):
    entities, width = emb_table.shape
    owners, slots = send_rows.shape[2:]
    columns = lax.axis_size("bucket")
    packed = (owners, (CHUNKS - 1) * slots + slots // 4, LANES)
    send = send_rows.reshape(owners * slots)
    table = emb_table.T
    own_negs = pl.pallas_call(
        negs_kernel,
        out_shape=shaped(columns // 4, 16, LANES),
        in_specs=[VMEM, VMEM],
        out_specs=VMEM,
        scratch_shapes=[in_vmem(WIDE, entities)],
        name="negs",
    )(neg_rows, table)
    picked = pl.pallas_call(
        pick_kernel,
        out_shape=shaped(*packed),
        in_specs=[VMEM, VMEM],
        out_specs=VMEM,
        scratch_shapes=[in_vmem(WIDE, entities)],
        name="pick",
    )(send[:, None], table)
    negs = gather_columns(own_negs, columns)
    got = lax.all_to_all(picked, "dom", split_axis=0, concat_axis=0, tiled=True)
    ends = jnp.concatenate([src_slot.reshape(-1), dst_slot.reshape(-1)])
    relation = jnp.pad(rel_diag[block_rel.reshape(-1)], ((0, 0), (0, WIDE - width)))
    back, negs_back = pl.pallas_call(
        grad_kernel,
        out_shape=(shaped(*packed), in_vmem(columns * 16, LANES)),
        in_specs=[VMEM] * 5,
        out_specs=(VMEM, VMEM),
        scratch_shapes=[
            in_vmem(owners * slots, WIDE),
            in_vmem(2 * columns, WIDE),
            in_vmem(ends.shape[0], WIDE),
        ],
        name="grad",
    )(ends[:, None], ends[None, :], relation, near(got), near(negs.reshape(columns * 16, LANES)))
    own_grad = sum_columns(negs_back, columns)
    returned = lax.all_to_all(back, "dom", split_axis=0, concat_axis=0, tiled=True)
    put = pl.pallas_call(
        put_kernel,
        out_shape=in_vmem(WIDE, entities),
        in_specs=[VMEM, VMEM],
        out_specs=VMEM,
        scratch_shapes=[in_vmem(owners * slots, WIDE)],
        name="put",
    )(send[None, :], near(returned))
    return pl.pallas_call(
        add_kernel,
        out_shape=shaped(width, entities),
        in_specs=[VMEM, VMEM, VMEM],
        out_specs=VMEM,
        name="add",
    )(neg_rows, near(put), near(own_grad)).T


def solution(mesh):
    placed = (
        P(("dom", "bucket"), None),
        P(),
        P("dom", "bucket", None, None),
        P("dom", "bucket", None),
        P("dom", "bucket", None),
        P("dom", "bucket", None, None),
        P("dom", "bucket", None),
    )
    return jax.shard_map(
        on_device, mesh=mesh, in_specs=placed, out_specs=P(("dom", "bucket"), None), check_vma=False
    )
```

```python
import functools

import jax
import jax.numpy as jnp
from jax import lax
from jax.experimental import pallas as pl
from jax.experimental.pallas import tpu as pltpu
from jax.sharding import PartitionSpec as P

LANES = 128
CHUNKS = 4
TAIL = 16
WIDE = CHUNKS * LANES
UNIT = 13
HIGHEST = lax.Precision.HIGHEST
VMEM = pl.BlockSpec(memory_space=pltpu.VMEM)


def split(x, terms):
    parts = []
    for _ in range(terms):
        part = x.astype(jnp.bfloat16)
        parts.append(part)
        x = x - part.astype(jnp.float32)
    return parts


def select_rows(onehot, x, terms):
    total = None
    for part in split(x, terms):
        product = jnp.dot(onehot, part, preferred_element_type=jnp.float32)
        total = product if total is None else total + product
    return total


def product(a, b):
    (a_high, a_low), (b_high, b_low) = split(a, 2), split(b, 2)
    dot = lambda x, y: jnp.dot(x, y, preferred_element_type=jnp.float32)
    return dot(a_high, b_high) + (dot(a_high, b_low) + dot(a_low, b_high))


def onehot_of(index, shape, axis):
    return jnp.where(index == lax.broadcasted_iota(jnp.int32, shape, axis), 1.0, 0.0).astype(jnp.bfloat16)


def pack(x, out_ref):
    owners = out_ref.shape[0]
    slots = x.shape[0] // owners
    group = slots // 4
    for j in range(CHUNKS - 1):
        out_ref[:, j * slots : (j + 1) * slots, :] = x[:, j * LANES : (j + 1) * LANES].reshape(owners, slots, LANES)
    tails = x[:, (CHUNKS - 1) * LANES :].reshape(owners, 4, group, LANES)
    tail = tails[:, 0].reshape(owners * group, LANES)
    for q in range(1, 4):
        tail = tail + pltpu.roll(tails[:, q].reshape(owners * group, LANES), TAIL * q, 1)
    out_ref[:, (CHUNKS - 1) * slots :, :] = tail.reshape(owners, group, LANES)


def unpack(ref, out_ref):
    owners = ref.shape[0]
    slots = out_ref.shape[0] // owners
    group = slots // 4
    for j in range(CHUNKS - 1):
        out_ref[:, j * LANES : (j + 1) * LANES] = ref[:, j * slots : (j + 1) * slots, :].reshape(owners * slots, LANES)
    tail = ref[:, (CHUNKS - 1) * slots :, :].reshape(owners * group, LANES)
    live = lax.broadcasted_iota(jnp.int32, tail.shape, 1) < TAIL
    tails = []
    for q in range(4):
        turned = tail if q == 0 else pltpu.roll(tail, LANES - TAIL * q, 1)
        tails.append(jnp.where(live, turned, 0.0).reshape(owners, group, LANES))
    out_ref[:, (CHUNKS - 1) * LANES :] = jnp.stack(tails, axis=1).reshape(owners * slots, LANES)


def widen(ref, out_ref):
    width = ref.shape[0]
    out_ref[:width, :] = ref[...]
    out_ref[width:, :] = jnp.zeros((out_ref.shape[0] - width, out_ref.shape[1]), jnp.float32)


def select_columns(onehot, x, terms):
    total = None
    for part in split(x, terms):
        product = lax.dot_general(onehot, part, (((1,), (1,)), ((), ())), preferred_element_type=jnp.float32)
        total = product if total is None else total + product
    return total


def own_row(neg_ref, n):
    return neg_ref[0, 0, n // 2 : n // 2 + 1, n % 2 : n % 2 + 1]


def negs_kernel(neg_ref, table_ref, out_ref, table):
    widen(table_ref, table)
    entities = table.shape[1]
    place = lax.broadcasted_iota(jnp.int32, (8, entities), 0)
    entity = lax.broadcasted_iota(jnp.int32, (8, entities), 1)
    hit = jnp.zeros((8, entities), jnp.float32)
    for n in range(4):
        hit = jnp.where((place == n) & (entity == own_row(neg_ref, n)), 1.0, hit)
    rows = select_columns(hit.astype(jnp.bfloat16), table[...], 3)
    for j in range(CHUNKS):
        part = rows[:4, j * LANES : (j + 1) * LANES]
        out_ref[:, j * 4 : j * 4 + 4, :] = jnp.broadcast_to(part, (out_ref.shape[0], 4, LANES))


def pick_kernel(send_ref, table_ref, rows_ref, table):
    widen(table_ref, table)
    onehot = onehot_of(send_ref[...], (send_ref.shape[0], table.shape[1]), 1)
    pack(select_columns(onehot, table[...], 3), rows_ref)


def grad_kernel(col_ref, row_ref, rel_ref, got_ref, negs_ref, back_ref, negs_back_ref, rows, negs, grads):
    unpack(got_ref, rows)
    slots, ends = rows.shape[0], col_ref.shape[0]
    edges = ends // 2
    blocks = rel_ref.shape[0]
    block = edges // blocks
    owners = negs_ref.shape[0] // 16
    tail = jnp.zeros((owners, LANES), jnp.float32)
    picked = select_rows(onehot_of(col_ref[...], (ends, slots), 1), rows[...], 3)
    for c in range(blocks):
        for k in range(2):
            for j in range(CHUNKS):
                negs[k * owners : (k + 1) * owners, j * LANES : (j + 1) * LANES] = negs_ref[
                    pl.ds(j * 4 + c * 2 + k, owners, stride=16), :
                ]
        negatives = negs[...]
        relation = rel_ref[c : c + 1, :]
        query = picked[c * block : (c + 1) * block] * relation
        target = picked[edges + c * block : edges + (c + 1) * block]
        positive = jnp.sum(query * target, axis=1, keepdims=True)
        scores = lax.dot_general(
            query, negatives, (((1,), (1,)), ((), ())), precision=HIGHEST, preferred_element_type=jnp.float32
        )
        largest = jnp.maximum(jnp.max(scores, axis=1, keepdims=True), positive)
        pos_exp = jnp.exp(positive - largest)
        neg_exp = jnp.exp(scores - largest)
        total = pos_exp + jnp.sum(neg_exp, axis=1, keepdims=True)
        pos_weight = pos_exp / total - 1.0
        weight = neg_exp / total
        query_grad = pos_weight * target + product(weight, negatives)
        grads[c * block : (c + 1) * block, :] = query_grad * relation
        grads[edges + c * block : edges + (c + 1) * block, :] = pos_weight * query
        neg_grad = product(weight.T, query)
        for k in range(2):
            n = c * 2 + k
            part = neg_grad[k * owners : (k + 1) * owners]
            for j in range(CHUNKS - 1):
                negs_back_ref[pl.ds(j * 4 + n, owners, stride=UNIT), :] = part[:, j * LANES : (j + 1) * LANES]
            last = part[:, (CHUNKS - 1) * LANES :]
            tail = tail + (pltpu.roll(last, TAIL * n, 1) if n else last)
    negs_back_ref[pl.ds(UNIT - 1, owners, stride=UNIT), :] = tail
    pack(select_rows(onehot_of(row_ref[...], (slots, ends), 0), grads[...], 2), back_ref)


def put_kernel(send_ref, got_ref, out_ref, rows):
    unpack(got_ref, rows)
    entities = out_ref.shape[1]
    out_ref[...] = select_rows(onehot_of(send_ref[...], (entities, rows.shape[0]), 0), rows[...], 2).T


def add_kernel(neg_ref, put_ref, parts_ref, out_ref, total, sems):
    own = jnp.sum(parts_ref[...], axis=0).T
    width, entities = out_ref.shape
    copies = []
    for j in range(CHUNKS):
        stop = min(width, (j + 1) * LANES) - j * LANES
        part = put_ref[j * LANES : j * LANES + stop, :]
        entity = lax.broadcasted_iota(jnp.int32, part.shape, 1)
        for n in range(4):
            if stop == LANES:
                own_part = own[:, j * 4 + n : j * 4 + n + 1]
            else:
                own_part = own[TAIL * n : TAIL * n + stop, UNIT - 1 : UNIT]
            part = part + jnp.where(entity == own_row(neg_ref, n), own_part, 0.0)
        rows = pl.ds(j * LANES, stop)
        total[rows, :] = part
        copies.append(pltpu.make_async_copy(total.at[rows], out_ref.at[rows], sems.at[j]))
        copies[-1].start()
    for copy in copies:
        copy.wait()


def near(x):
    return pltpu.with_memory_space_constraint(x, pltpu.VMEM)


def shaped(*shape):
    return jax.ShapeDtypeStruct(shape, jnp.float32)


def in_vmem(*shape):
    return pltpu.VMEM(shape, jnp.float32)


def quarters(columns):
    side = 1
    while side * side < columns:
        side *= 2
    depth = columns // side
    groups = [
        [y * side + z for y in range(top, top + depth // 2) for z in range(left, left + side // 2)]
        for top in (0, depth // 2)
        for left in (0, side // 2)
    ]

    def mirror(flip_y, flip_z):
        pairs = []
        for b in range(columns):
            y, z = divmod(b, side)
            pairs.append((b, (depth - 1 - y if flip_y else y) * side + (side - 1 - z if flip_z else z)))
        return pairs

    return groups, [mirror(False, True), mirror(True, False), mirror(True, True)]


def gather_columns(x, columns):
    groups, mirrors = quarters(columns)
    x = lax.all_to_all(x, "bucket", split_axis=0, concat_axis=0, axis_index_groups=groups, tiled=True)
    return jnp.stack([x] + [lax.ppermute(x, "bucket", pairs) for pairs in mirrors])


def sum_columns(x, columns):
    groups, mirrors = quarters(columns)
    x = x.reshape(4, len(groups[0]) * UNIT, LANES)
    both, up, across = [lax.ppermute(x[i], "bucket", mirrors[i - 1]) for i in (3, 2, 1)]
    x = ((both + up) + across) + x[0]
    x = x.reshape(len(groups[0]), UNIT, LANES)
    return lax.all_to_all(x, "bucket", split_axis=0, concat_axis=0, axis_index_groups=groups, tiled=True)


def on_device(emb_table, rel_diag, send_rows, src_slot, dst_slot, neg_rows, block_rel):
    entities, width = emb_table.shape
    owners, slots = send_rows.shape[2:]
    columns = lax.axis_size("bucket")
    packed = (owners, (CHUNKS - 1) * slots + slots // 4, LANES)
    send = send_rows.reshape(owners * slots)
    table = emb_table.T
    own_negs = pl.pallas_call(
        negs_kernel,
        out_shape=shaped(columns // 4, 16, LANES),
        in_specs=[VMEM, VMEM],
        out_specs=VMEM,
        scratch_shapes=[in_vmem(WIDE, entities)],
        name="negs",
    )(neg_rows, table)
    picked = pl.pallas_call(
        pick_kernel,
        out_shape=shaped(*packed),
        in_specs=[VMEM, VMEM],
        out_specs=VMEM,
        scratch_shapes=[in_vmem(WIDE, entities)],
        name="pick",
    )(send[:, None], table)
    negs = gather_columns(own_negs, columns)
    got = lax.all_to_all(picked, "dom", split_axis=0, concat_axis=0, tiled=True)
    ends = jnp.concatenate([src_slot.reshape(-1), dst_slot.reshape(-1)])
    relation = jnp.pad(rel_diag[block_rel.reshape(-1)], ((0, 0), (0, WIDE - width)))
    back, negs_back = pl.pallas_call(
        grad_kernel,
        out_shape=(shaped(*packed), in_vmem(columns * UNIT, LANES)),
        in_specs=[VMEM] * 5,
        out_specs=(VMEM, VMEM),
        scratch_shapes=[
            in_vmem(owners * slots, WIDE),
            in_vmem(2 * columns, WIDE),
            in_vmem(ends.shape[0], WIDE),
        ],
        name="grad",
    )(near(ends[:, None]), near(ends[None, :]), near(relation), near(got), near(negs.reshape(columns * 16, LANES)))
    own_grad = sum_columns(negs_back, columns)
    returned = lax.all_to_all(back, "dom", split_axis=0, concat_axis=0, tiled=True)
    put = pl.pallas_call(
        put_kernel,
        out_shape=in_vmem(WIDE, entities),
        in_specs=[VMEM, VMEM],
        out_specs=VMEM,
        scratch_shapes=[in_vmem(owners * slots, WIDE)],
        name="put",
    )(near(send[None, :]), near(returned))
    return pl.pallas_call(
        add_kernel,
        out_shape=shaped(width, entities),
        in_specs=[VMEM, VMEM, VMEM],
        out_specs=pl.BlockSpec(memory_space=pl.ANY),
        scratch_shapes=[in_vmem(width, entities), pltpu.SemaphoreType.DMA((CHUNKS,))],
        name="add",
    )(near(neg_rows), near(put), near(own_grad)).T


def solution(mesh):
    placed = (
        P(("dom", "bucket"), None),
        P(),
        P("dom", "bucket", None, None),
        P("dom", "bucket", None),
        P("dom", "bucket", None),
        P("dom", "bucket", None, None),
        P("dom", "bucket", None),
    )
    return jax.shard_map(
        on_device, mesh=mesh, in_specs=placed, out_specs=P(("dom", "bucket"), None), check_vma=False
    )
```

```python
import functools

import jax
import jax.numpy as jnp
from jax import lax
from jax.experimental import pallas as pl
from jax.experimental.pallas import tpu as pltpu
from jax.sharding import PartitionSpec as P

LANES = 128
CHUNKS = 4
TAIL = 16
WIDE = CHUNKS * LANES
UNIT = 13
HIGHEST = lax.Precision.HIGHEST
VMEM = pl.BlockSpec(memory_space=pltpu.VMEM)


def split(x, terms):
    parts = []
    for _ in range(terms):
        part = x.astype(jnp.bfloat16)
        parts.append(part)
        x = x - part.astype(jnp.float32)
    return parts


def select_rows(onehot, x, terms):
    total = None
    for part in split(x, terms):
        product = jnp.dot(onehot, part, preferred_element_type=jnp.float32)
        total = product if total is None else total + product
    return total


def product(a, b):
    (a_high, a_low), (b_high, b_low) = split(a, 2), split(b, 2)
    dot = lambda x, y: jnp.dot(x, y, preferred_element_type=jnp.float32)
    return dot(a_high, b_high) + (dot(a_high, b_low) + dot(a_low, b_high))


def onehot_of(index, shape, axis):
    return jnp.where(index == lax.broadcasted_iota(jnp.int32, shape, axis), 1.0, 0.0).astype(jnp.bfloat16)


def pack(x, out_ref):
    owners = out_ref.shape[0]
    slots = x.shape[0] // owners
    group = slots // 4
    for j in range(CHUNKS - 1):
        out_ref[:, j * slots : (j + 1) * slots, :] = x[:, j * LANES : (j + 1) * LANES].reshape(owners, slots, LANES)
    tails = x[:, (CHUNKS - 1) * LANES :].reshape(owners, 4, group, LANES)
    tail = tails[:, 0].reshape(owners * group, LANES)
    for q in range(1, 4):
        tail = tail + pltpu.roll(tails[:, q].reshape(owners * group, LANES), TAIL * q, 1)
    out_ref[:, (CHUNKS - 1) * slots :, :] = tail.reshape(owners, group, LANES)


def unpack(ref, out_ref):
    owners = ref.shape[0]
    slots = out_ref.shape[0] // owners
    group = slots // 4
    for j in range(CHUNKS - 1):
        out_ref[:, j * LANES : (j + 1) * LANES] = ref[:, j * slots : (j + 1) * slots, :].reshape(owners * slots, LANES)
    tail = ref[:, (CHUNKS - 1) * slots :, :].reshape(owners * group, LANES)
    live = lax.broadcasted_iota(jnp.int32, tail.shape, 1) < TAIL
    tails = []
    for q in range(4):
        turned = tail if q == 0 else pltpu.roll(tail, LANES - TAIL * q, 1)
        tails.append(jnp.where(live, turned, 0.0).reshape(owners, group, LANES))
    out_ref[:, (CHUNKS - 1) * LANES :] = jnp.stack(tails, axis=1).reshape(owners * slots, LANES)


def widen(ref, out_ref):
    width = ref.shape[0]
    out_ref[:width, :] = ref[...]
    out_ref[width:, :] = jnp.zeros((out_ref.shape[0] - width, out_ref.shape[1]), jnp.float32)


def select_columns(onehot, x, terms):
    total = None
    for part in split(x, terms):
        product = lax.dot_general(onehot, part, (((1,), (1,)), ((), ())), preferred_element_type=jnp.float32)
        total = product if total is None else total + product
    return total


def own_row(neg_ref, n):
    return neg_ref[0, 0, n // 2 : n // 2 + 1, n % 2 : n % 2 + 1]


def negs_kernel(neg_ref, table_ref, out_ref, table):
    widen(table_ref, table)
    entities = table.shape[1]
    place = lax.broadcasted_iota(jnp.int32, (8, entities), 0)
    entity = lax.broadcasted_iota(jnp.int32, (8, entities), 1)
    hit = jnp.zeros((8, entities), jnp.float32)
    for n in range(4):
        hit = jnp.where((place == n) & (entity == own_row(neg_ref, n)), 1.0, hit)
    rows = select_columns(hit.astype(jnp.bfloat16), table[...], 3)
    for j in range(CHUNKS - 1):
        part = rows[:4, j * LANES : (j + 1) * LANES]
        out_ref[:, j * 4 : j * 4 + 4, :] = jnp.broadcast_to(part, (out_ref.shape[0], 4, LANES))
    last = rows[:, (CHUNKS - 1) * LANES :]
    tail = last[:1]
    for n in range(1, 4):
        tail = tail + pltpu.roll(last, TAIL * n, 1)[n : n + 1]
    out_ref[:, UNIT - 1 : UNIT, :] = jnp.broadcast_to(tail, (out_ref.shape[0], 1, LANES))


def pick_kernel(send_ref, table_ref, rows_ref, table):
    widen(table_ref, table)
    onehot = onehot_of(send_ref[...], (send_ref.shape[0], table.shape[1]), 1)
    pack(select_columns(onehot, table[...], 3), rows_ref)


def grad_kernel(col_ref, row_ref, rel_ref, got_ref, negs_ref, back_ref, negs_back_ref, rows, negs, grads):
    unpack(got_ref, rows)
    slots, ends = rows.shape[0], col_ref.shape[0]
    edges = ends // 2
    blocks = rel_ref.shape[0]
    block = edges // blocks
    owners = negs_ref.shape[0] // UNIT
    tails = negs_ref[pl.ds(UNIT - 1, owners, stride=UNIT), :]
    live = lax.broadcasted_iota(jnp.int32, tails.shape, 1) < TAIL
    tail = jnp.zeros((owners, LANES), jnp.float32)
    picked = select_rows(onehot_of(col_ref[...], (ends, slots), 1), rows[...], 3)
    for c in range(blocks):
        for k in range(2):
            n = c * 2 + k
            for j in range(CHUNKS - 1):
                negs[k * owners : (k + 1) * owners, j * LANES : (j + 1) * LANES] = negs_ref[
                    pl.ds(j * 4 + n, owners, stride=UNIT), :
                ]
            turned = pltpu.roll(tails, LANES - TAIL * n, 1) if n else tails
            negs[k * owners : (k + 1) * owners, (CHUNKS - 1) * LANES :] = jnp.where(live, turned, 0.0)
        negatives = negs[...]
        relation = rel_ref[c : c + 1, :]
        query = picked[c * block : (c + 1) * block] * relation
        target = picked[edges + c * block : edges + (c + 1) * block]
        positive = jnp.sum(query * target, axis=1, keepdims=True)
        scores = lax.dot_general(
            query, negatives, (((1,), (1,)), ((), ())), precision=HIGHEST, preferred_element_type=jnp.float32
        )
        largest = jnp.maximum(jnp.max(scores, axis=1, keepdims=True), positive)
        pos_exp = jnp.exp(positive - largest)
        neg_exp = jnp.exp(scores - largest)
        total = pos_exp + jnp.sum(neg_exp, axis=1, keepdims=True)
        pos_weight = pos_exp / total - 1.0
        weight = neg_exp / total
        query_grad = pos_weight * target + product(weight, negatives)
        grads[c * block : (c + 1) * block, :] = query_grad * relation
        grads[edges + c * block : edges + (c + 1) * block, :] = pos_weight * query
        neg_grad = product(weight.T, query)
        for k in range(2):
            n = c * 2 + k
            part = neg_grad[k * owners : (k + 1) * owners]
            for j in range(CHUNKS - 1):
                negs_back_ref[pl.ds(j * 4 + n, owners, stride=UNIT), :] = part[:, j * LANES : (j + 1) * LANES]
            last = part[:, (CHUNKS - 1) * LANES :]
            tail = tail + (pltpu.roll(last, TAIL * n, 1) if n else last)
    negs_back_ref[pl.ds(UNIT - 1, owners, stride=UNIT), :] = tail
    pack(select_rows(onehot_of(row_ref[...], (slots, ends), 0), grads[...], 2), back_ref)


def put_kernel(send_ref, got_ref, out_ref, rows):
    unpack(got_ref, rows)
    entities = out_ref.shape[1]
    out_ref[...] = select_rows(onehot_of(send_ref[...], (entities, rows.shape[0]), 0), rows[...], 2).T


def add_kernel(neg_ref, put_ref, parts_ref, out_ref, total, sems):
    own = jnp.sum(parts_ref[...], axis=0).T
    width, entities = out_ref.shape
    copies = []
    for j in range(CHUNKS):
        stop = min(width, (j + 1) * LANES) - j * LANES
        part = put_ref[j * LANES : j * LANES + stop, :]
        entity = lax.broadcasted_iota(jnp.int32, part.shape, 1)
        for n in range(4):
            if stop == LANES:
                own_part = own[:, j * 4 + n : j * 4 + n + 1]
            else:
                own_part = own[TAIL * n : TAIL * n + stop, UNIT - 1 : UNIT]
            part = part + jnp.where(entity == own_row(neg_ref, n), own_part, 0.0)
        rows = pl.ds(j * LANES, stop)
        total[rows, :] = part
        copies.append(pltpu.make_async_copy(total.at[rows], out_ref.at[rows], sems.at[j]))
        copies[-1].start()
    for copy in copies:
        copy.wait()


def near(x):
    return pltpu.with_memory_space_constraint(x, pltpu.VMEM)


def shaped(*shape):
    return jax.ShapeDtypeStruct(shape, jnp.float32)


def in_vmem(*shape):
    return pltpu.VMEM(shape, jnp.float32)


def quarters(columns):
    side = 1
    while side * side < columns:
        side *= 2
    depth = columns // side
    groups = [
        [y * side + z for y in range(top, top + depth // 2) for z in range(left, left + side // 2)]
        for top in (0, depth // 2)
        for left in (0, side // 2)
    ]

    def mirror(flip_y, flip_z):
        pairs = []
        for b in range(columns):
            y, z = divmod(b, side)
            pairs.append((b, (depth - 1 - y if flip_y else y) * side + (side - 1 - z if flip_z else z)))
        return pairs

    return groups, [mirror(False, True), mirror(True, False), mirror(True, True)]


def gather_columns(x, columns, later):
    groups, mirrors = quarters(columns)
    x = lax.all_to_all(x, "bucket", split_axis=0, concat_axis=0, axis_index_groups=groups, tiled=True)
    x, later = lax.optimization_barrier((x.reshape(len(groups[0]) * UNIT, LANES), later))
    return jnp.stack([x] + [lax.ppermute(x, "bucket", pairs) for pairs in mirrors]), later


def sum_columns(x, columns):
    groups, mirrors = quarters(columns)
    x = x.reshape(4, len(groups[0]) * UNIT, LANES)
    both, up, across = [lax.ppermute(x[i], "bucket", mirrors[i - 1]) for i in (3, 2, 1)]
    x = ((both + up) + across) + x[0]
    x = x.reshape(len(groups[0]), UNIT, LANES)
    return lax.all_to_all(x, "bucket", split_axis=0, concat_axis=0, axis_index_groups=groups, tiled=True)


def on_device(emb_table, rel_diag, send_rows, src_slot, dst_slot, neg_rows, block_rel):
    entities, width = emb_table.shape
    owners, slots = send_rows.shape[2:]
    columns = lax.axis_size("bucket")
    packed = (owners, (CHUNKS - 1) * slots + slots // 4, LANES)
    send = send_rows.reshape(owners * slots)
    table = emb_table.T
    own_negs = pl.pallas_call(
        negs_kernel,
        out_shape=shaped(columns // 4, UNIT, LANES),
        in_specs=[VMEM, VMEM],
        out_specs=VMEM,
        scratch_shapes=[in_vmem(WIDE, entities)],
        name="negs",
    )(neg_rows, table)
    picked = pl.pallas_call(
        pick_kernel,
        out_shape=shaped(*packed),
        in_specs=[VMEM, VMEM],
        out_specs=VMEM,
        scratch_shapes=[in_vmem(WIDE, entities)],
        name="pick",
    )(near(send[:, None]), near(table))
    negs, (sources, targets, kinds) = gather_columns(own_negs, columns, (src_slot, dst_slot, block_rel))
    got = lax.all_to_all(picked, "dom", split_axis=0, concat_axis=0, tiled=True)
    ends = jnp.concatenate([sources.reshape(-1), targets.reshape(-1)])
    relation = jnp.pad(rel_diag[kinds.reshape(-1)], ((0, 0), (0, WIDE - width)))
    back, negs_back = pl.pallas_call(
        grad_kernel,
        out_shape=(shaped(*packed), in_vmem(columns * UNIT, LANES)),
        in_specs=[VMEM] * 5,
        out_specs=(VMEM, VMEM),
        scratch_shapes=[
            in_vmem(owners * slots, WIDE),
            in_vmem(2 * columns, WIDE),
            in_vmem(ends.shape[0], WIDE),
        ],
        name="grad",
    )(near(ends[:, None]), near(ends[None, :]), near(relation), near(got), near(negs.reshape(columns * UNIT, LANES)))
    own_grad = sum_columns(negs_back, columns)
    returned = lax.all_to_all(back, "dom", split_axis=0, concat_axis=0, tiled=True)
    put = pl.pallas_call(
        put_kernel,
        out_shape=in_vmem(WIDE, entities),
        in_specs=[VMEM, VMEM],
        out_specs=VMEM,
        scratch_shapes=[in_vmem(owners * slots, WIDE)],
        name="put",
    )(near(send[None, :]), near(returned))
    return pl.pallas_call(
        add_kernel,
        out_shape=shaped(width, entities),
        in_specs=[VMEM, VMEM, VMEM],
        out_specs=pl.BlockSpec(memory_space=pl.ANY),
        scratch_shapes=[in_vmem(width, entities), pltpu.SemaphoreType.DMA((CHUNKS,))],
        name="add",
    )(near(neg_rows), near(put), near(own_grad)).T


def solution(mesh):
    placed = (
        P(("dom", "bucket"), None),
        P(),
        P("dom", "bucket", None, None),
        P("dom", "bucket", None),
        P("dom", "bucket", None),
        P("dom", "bucket", None, None),
        P("dom", "bucket", None),
    )
    return jax.shard_map(
        on_device, mesh=mesh, in_specs=placed, out_specs=P(("dom", "bucket"), None), check_vma=False
    )
```

```python
import functools

import jax
import jax.numpy as jnp
from jax import lax
from jax.experimental import pallas as pl
from jax.experimental.pallas import tpu as pltpu
from jax.sharding import PartitionSpec as P

LANES = 128
CHUNKS = 4
TAIL = 16
WIDE = CHUNKS * LANES
UNIT = 13
VMEM = pl.BlockSpec(memory_space=pltpu.VMEM)


def split(x, terms):
    parts = []
    for _ in range(terms):
        part = x.astype(jnp.bfloat16)
        parts.append(part)
        x = x - part.astype(jnp.float32)
    return parts


def select_rows(onehot, x, terms):
    total = None
    for part in split(x, terms):
        product = jnp.dot(onehot, part, preferred_element_type=jnp.float32)
        total = product if total is None else total + product
    return total


def dot_terms(a, b, contract, pairs):
    total = None
    for i, j in pairs:
        part = lax.dot_general(a[i], b[j], (contract, ((), ())), preferred_element_type=jnp.float32)
        total = part if total is None else total + part
    return total


NEAR = ((0, 1), (1, 0), (0, 0))
FULL = ((1, 1), (0, 2), (2, 0), (0, 1), (1, 0), (0, 0))


def onehot_of(index, shape, axis):
    return jnp.where(index == lax.broadcasted_iota(jnp.int32, shape, axis), 1.0, 0.0).astype(jnp.bfloat16)


def pack(x, out_ref):
    owners = out_ref.shape[0]
    slots = x.shape[0] // owners
    group = slots // 4
    for j in range(CHUNKS - 1):
        out_ref[:, j * slots : (j + 1) * slots, :] = x[:, j * LANES : (j + 1) * LANES].reshape(owners, slots, LANES)
    tails = x[:, (CHUNKS - 1) * LANES :].reshape(owners, 4, group, LANES)
    tail = tails[:, 0].reshape(owners * group, LANES)
    for q in range(1, 4):
        tail = tail + pltpu.roll(tails[:, q].reshape(owners * group, LANES), TAIL * q, 1)
    out_ref[:, (CHUNKS - 1) * slots :, :] = tail.reshape(owners, group, LANES)


def unpack(ref, out_ref):
    owners = ref.shape[0]
    slots = out_ref.shape[0] // owners
    group = slots // 4
    for j in range(CHUNKS - 1):
        out_ref[:, j * LANES : (j + 1) * LANES] = ref[:, j * slots : (j + 1) * slots, :].reshape(owners * slots, LANES)
    tail = ref[:, (CHUNKS - 1) * slots :, :].reshape(owners * group, LANES)
    live = lax.broadcasted_iota(jnp.int32, tail.shape, 1) < TAIL
    tails = []
    for q in range(4):
        turned = tail if q == 0 else pltpu.roll(tail, LANES - TAIL * q, 1)
        tails.append(jnp.where(live, turned, 0.0).reshape(owners, group, LANES))
    out_ref[:, (CHUNKS - 1) * LANES :] = jnp.stack(tails, axis=1).reshape(owners * slots, LANES)


def widen(ref, out_ref):
    width = ref.shape[0]
    out_ref[:width, :] = ref[...]
    out_ref[width:, :] = jnp.zeros((out_ref.shape[0] - width, out_ref.shape[1]), jnp.float32)


def select_columns(onehot, x, terms):
    total = None
    for part in split(x, terms):
        product = lax.dot_general(onehot, part, (((1,), (1,)), ((), ())), preferred_element_type=jnp.float32)
        total = product if total is None else total + product
    return total


def own_row(neg_ref, n):
    return neg_ref[0, 0, n // 2 : n // 2 + 1, n % 2 : n % 2 + 1]


def negs_kernel(neg_ref, table_ref, out_ref, table):
    widen(table_ref, table)
    entities = table.shape[1]
    place = lax.broadcasted_iota(jnp.int32, (8, entities), 0)
    entity = lax.broadcasted_iota(jnp.int32, (8, entities), 1)
    hit = jnp.zeros((8, entities), jnp.float32)
    for n in range(4):
        hit = jnp.where((place == n) & (entity == own_row(neg_ref, n)), 1.0, hit)
    rows = select_columns(hit.astype(jnp.bfloat16), table[...], 3)
    for j in range(CHUNKS - 1):
        part = rows[:4, j * LANES : (j + 1) * LANES]
        out_ref[:, j * 4 : j * 4 + 4, :] = jnp.broadcast_to(part, (out_ref.shape[0], 4, LANES))
    last = rows[:, (CHUNKS - 1) * LANES :]
    tail = last[:1]
    for n in range(1, 4):
        tail = tail + pltpu.roll(last, TAIL * n, 1)[n : n + 1]
    out_ref[:, UNIT - 1 : UNIT, :] = jnp.broadcast_to(tail, (out_ref.shape[0], 1, LANES))


def pick_kernel(send_ref, table_ref, rows_ref, table):
    widen(table_ref, table)
    onehot = onehot_of(send_ref[...], (send_ref.shape[0], table.shape[1]), 1)
    pack(select_columns(onehot, table[...], 3), rows_ref)


def grad_kernel(col_ref, row_ref, rel_ref, got_ref, negs_ref, back_ref, negs_back_ref, rows, negs, grads):
    unpack(got_ref, rows)
    slots, ends = rows.shape[0], col_ref.shape[0]
    edges = ends // 2
    blocks = rel_ref.shape[0]
    block = edges // blocks
    owners = negs_ref.shape[0] // UNIT
    tails = negs_ref[pl.ds(UNIT - 1, owners, stride=UNIT), :]
    live = lax.broadcasted_iota(jnp.int32, tails.shape, 1) < TAIL
    tail = jnp.zeros((owners, LANES), jnp.float32)
    picked = select_rows(onehot_of(col_ref[...], (ends, slots), 1), rows[...], 3)
    for c in range(blocks):
        for k in range(2):
            n = c * 2 + k
            for j in range(CHUNKS - 1):
                negs[c, k * owners : (k + 1) * owners, j * LANES : (j + 1) * LANES] = negs_ref[
                    pl.ds(j * 4 + n, owners, stride=UNIT), :
                ]
            turned = pltpu.roll(tails, LANES - TAIL * n, 1) if n else tails
            negs[c, k * owners : (k + 1) * owners, (CHUNKS - 1) * LANES :] = jnp.where(live, turned, 0.0)
    every = range(blocks)
    relation = [rel_ref[c : c + 1, :] for c in every]
    query = [picked[c * block : (c + 1) * block] * relation[c] for c in every]
    target = [picked[edges + c * block : edges + (c + 1) * block] for c in every]
    query_terms = [split(query[c], 3) for c in every]
    negative_terms = [split(negs[c], 3) for c in every]
    scores = [dot_terms(query_terms[c], negative_terms[c], ((1,), (1,)), FULL) for c in every]
    positive = [jnp.sum(query[c] * target[c], axis=1, keepdims=True) for c in every]
    largest = [jnp.maximum(jnp.max(scores[c], axis=1, keepdims=True), positive[c]) for c in every]
    pos_exp = [jnp.exp(positive[c] - largest[c]) for c in every]
    neg_exp = [jnp.exp(scores[c] - largest[c]) for c in every]
    total = [pos_exp[c] + jnp.sum(neg_exp[c], axis=1, keepdims=True) for c in every]
    pos_weight = [pos_exp[c] / total[c] - 1.0 for c in every]
    weight = [neg_exp[c] / total[c] for c in every]
    pulled = [dot_terms(split(weight[c], 2), negative_terms[c], ((1,), (0,)), NEAR) for c in every]
    pushed = [dot_terms(split(weight[c].T, 2), query_terms[c], ((1,), (0,)), NEAR) for c in every]
    for c in every:
        grads[c * block : (c + 1) * block, :] = (pos_weight[c] * target[c] + pulled[c]) * relation[c]
        grads[edges + c * block : edges + (c + 1) * block, :] = pos_weight[c] * query[c]
    for c in every:
        for k in range(2):
            n = c * 2 + k
            part = pushed[c][k * owners : (k + 1) * owners]
            for j in range(CHUNKS - 1):
                negs_back_ref[pl.ds(j * 4 + n, owners, stride=UNIT), :] = part[:, j * LANES : (j + 1) * LANES]
            last = part[:, (CHUNKS - 1) * LANES :]
            tail = tail + (pltpu.roll(last, TAIL * n, 1) if n else last)
    negs_back_ref[pl.ds(UNIT - 1, owners, stride=UNIT), :] = tail
    pack(select_rows(onehot_of(row_ref[...], (slots, ends), 0), grads[...], 2), back_ref)


def put_kernel(send_ref, got_ref, out_ref, rows):
    unpack(got_ref, rows)
    entities = out_ref.shape[1]
    out_ref[...] = select_rows(onehot_of(send_ref[...], (entities, rows.shape[0]), 0), rows[...], 2).T


def add_kernel(neg_ref, put_ref, parts_ref, out_ref, total, sems):
    own = jnp.sum(parts_ref[...], axis=0).T
    width, entities = out_ref.shape
    copies = []
    for j in range(CHUNKS):
        stop = min(width, (j + 1) * LANES) - j * LANES
        part = put_ref[j * LANES : j * LANES + stop, :]
        entity = lax.broadcasted_iota(jnp.int32, part.shape, 1)
        for n in range(4):
            if stop == LANES:
                own_part = own[:, j * 4 + n : j * 4 + n + 1]
            else:
                own_part = own[TAIL * n : TAIL * n + stop, UNIT - 1 : UNIT]
            part = part + jnp.where(entity == own_row(neg_ref, n), own_part, 0.0)
        rows = pl.ds(j * LANES, stop)
        total[rows, :] = part
        copies.append(pltpu.make_async_copy(total.at[rows], out_ref.at[rows], sems.at[j]))
        copies[-1].start()
    for copy in copies:
        copy.wait()


def near(x):
    return pltpu.with_memory_space_constraint(x, pltpu.VMEM)


def shaped(*shape):
    return jax.ShapeDtypeStruct(shape, jnp.float32)


def in_vmem(*shape):
    return pltpu.VMEM(shape, jnp.float32)


def quarters(columns):
    side = 1
    while side * side < columns:
        side *= 2
    depth = columns // side
    groups = [
        [y * side + z for y in range(top, top + depth // 2) for z in range(left, left + side // 2)]
        for top in (0, depth // 2)
        for left in (0, side // 2)
    ]

    def mirror(flip_y, flip_z):
        pairs = []
        for b in range(columns):
            y, z = divmod(b, side)
            pairs.append((b, (depth - 1 - y if flip_y else y) * side + (side - 1 - z if flip_z else z)))
        return pairs

    return groups, [mirror(False, True), mirror(True, False), mirror(True, True)]


def gather_columns(x, columns, later):
    groups, mirrors = quarters(columns)
    x = lax.all_to_all(x, "bucket", split_axis=0, concat_axis=0, axis_index_groups=groups, tiled=True)
    x, later = lax.optimization_barrier((x.reshape(len(groups[0]) * UNIT, LANES), later))
    return jnp.stack([x] + [lax.ppermute(x, "bucket", pairs) for pairs in mirrors]), later


def sum_columns(x, columns):
    groups, mirrors = quarters(columns)
    x = x.reshape(4, len(groups[0]) * UNIT, LANES)
    both, up, across = [lax.ppermute(x[i], "bucket", mirrors[i - 1]) for i in (3, 2, 1)]
    x = ((both + up) + across) + x[0]
    x = x.reshape(len(groups[0]), UNIT, LANES)
    return lax.all_to_all(x, "bucket", split_axis=0, concat_axis=0, axis_index_groups=groups, tiled=True)


def on_device(emb_table, rel_diag, send_rows, src_slot, dst_slot, neg_rows, block_rel):
    entities, width = emb_table.shape
    owners, slots = send_rows.shape[2:]
    columns = lax.axis_size("bucket")
    packed = (owners, (CHUNKS - 1) * slots + slots // 4, LANES)
    send = send_rows.reshape(owners * slots)
    table = emb_table.T
    own_negs = pl.pallas_call(
        negs_kernel,
        out_shape=shaped(columns // 4, UNIT, LANES),
        in_specs=[VMEM, VMEM],
        out_specs=VMEM,
        scratch_shapes=[in_vmem(WIDE, entities)],
        name="negs",
    )(neg_rows, table)
    picked = pl.pallas_call(
        pick_kernel,
        out_shape=shaped(*packed),
        in_specs=[VMEM, VMEM],
        out_specs=VMEM,
        scratch_shapes=[in_vmem(WIDE, entities)],
        name="pick",
    )(near(send[:, None]), near(table))
    negs, (sources, targets, kinds) = gather_columns(own_negs, columns, (src_slot, dst_slot, block_rel))
    got = lax.all_to_all(picked, "dom", split_axis=0, concat_axis=0, tiled=True)
    ends = jnp.concatenate([sources.reshape(-1), targets.reshape(-1)])
    relation = jnp.pad(rel_diag[kinds.reshape(-1)], ((0, 0), (0, WIDE - width)))
    back, negs_back = pl.pallas_call(
        grad_kernel,
        out_shape=(shaped(*packed), in_vmem(columns * UNIT, LANES)),
        in_specs=[VMEM] * 5,
        out_specs=(VMEM, VMEM),
        scratch_shapes=[
            in_vmem(owners * slots, WIDE),
            in_vmem(block_rel.shape[2], 2 * columns, WIDE),
            in_vmem(ends.shape[0], WIDE),
        ],
        name="grad",
    )(near(ends[:, None]), near(ends[None, :]), near(relation), near(got), near(negs.reshape(columns * UNIT, LANES)))
    own_grad = sum_columns(negs_back, columns)
    returned = lax.all_to_all(back, "dom", split_axis=0, concat_axis=0, tiled=True)
    put = pl.pallas_call(
        put_kernel,
        out_shape=in_vmem(WIDE, entities),
        in_specs=[VMEM, VMEM],
        out_specs=VMEM,
        scratch_shapes=[in_vmem(owners * slots, WIDE)],
        name="put",
    )(near(send[None, :]), near(returned))
    return pl.pallas_call(
        add_kernel,
        out_shape=shaped(width, entities),
        in_specs=[VMEM, VMEM, VMEM],
        out_specs=pl.BlockSpec(memory_space=pl.ANY),
        scratch_shapes=[in_vmem(width, entities), pltpu.SemaphoreType.DMA((CHUNKS,))],
        name="add",
    )(near(neg_rows), near(put), near(own_grad)).T


def solution(mesh):
    placed = (
        P(("dom", "bucket"), None),
        P(),
        P("dom", "bucket", None, None),
        P("dom", "bucket", None),
        P("dom", "bucket", None),
        P("dom", "bucket", None, None),
        P("dom", "bucket", None),
    )
    return jax.shard_map(
        on_device, mesh=mesh, in_specs=placed, out_specs=P(("dom", "bucket"), None), check_vma=False
    )
```

```python
import functools

import jax
import jax.numpy as jnp
from jax import lax
from jax.experimental import pallas as pl
from jax.experimental.pallas import tpu as pltpu
from jax.sharding import PartitionSpec as P

LANES = 128
CHUNKS = 4
TAIL = 16
WIDE = CHUNKS * LANES
UNIT = 13
VMEM = pl.BlockSpec(memory_space=pltpu.VMEM)


def split(x, terms):
    parts = []
    for _ in range(terms):
        part = x.astype(jnp.bfloat16)
        parts.append(part)
        x = x - part.astype(jnp.float32)
    return parts


def select_rows(onehot, x, terms):
    total = None
    for part in split(x, terms):
        product = jnp.dot(onehot, part, preferred_element_type=jnp.float32)
        total = product if total is None else total + product
    return total


def dot_terms(a, b, contract, pairs):
    total = None
    for i, j in pairs:
        part = lax.dot_general(a[i], b[j], (contract, ((), ())), preferred_element_type=jnp.float32)
        total = part if total is None else total + part
    return total


NEAR = ((0, 1), (1, 0), (0, 0))
FULL = ((1, 1), (0, 2), (2, 0), (0, 1), (1, 0), (0, 0))


def onehot_of(index, shape, axis):
    return jnp.where(index == lax.broadcasted_iota(jnp.int32, shape, axis), 1.0, 0.0).astype(jnp.bfloat16)


def pack(x, out_ref):
    owners = out_ref.shape[0]
    slots = x.shape[0] // owners
    group = slots // 4
    for j in range(CHUNKS - 1):
        out_ref[:, j * slots : (j + 1) * slots, :] = x[:, j * LANES : (j + 1) * LANES].reshape(owners, slots, LANES)
    tails = x[:, (CHUNKS - 1) * LANES :].reshape(owners, 4, group, LANES)
    tail = tails[:, 0].reshape(owners * group, LANES)
    for q in range(1, 4):
        tail = tail + pltpu.roll(tails[:, q].reshape(owners * group, LANES), TAIL * q, 1)
    half = group // 2
    low = tail.reshape(owners, group, LANES)
    high = pltpu.roll(tail, LANES // 2, 1).reshape(owners, group, LANES)
    out_ref[:, (CHUNKS - 1) * slots :, :] = low[:, :half] + high[:, half:]


def unpack(ref, out_ref):
    owners = ref.shape[0]
    slots = out_ref.shape[0] // owners
    group = slots // 4
    for j in range(CHUNKS - 1):
        out_ref[:, j * LANES : (j + 1) * LANES] = ref[:, j * slots : (j + 1) * slots, :].reshape(owners * slots, LANES)
    low = ref[:, (CHUNKS - 1) * slots :, :]
    high = jnp.concatenate([low[:, :, LANES // 2 :], low[:, :, : LANES // 2]], axis=2)
    tail = jnp.concatenate([low, high], axis=1).reshape(owners * group, LANES)
    live = lax.broadcasted_iota(jnp.int32, tail.shape, 1) < TAIL
    tails = []
    for q in range(4):
        turned = tail if q == 0 else pltpu.roll(tail, LANES - TAIL * q, 1)
        tails.append(jnp.where(live, turned, 0.0).reshape(owners, group, LANES))
    out_ref[:, (CHUNKS - 1) * LANES :] = jnp.stack(tails, axis=1).reshape(owners * slots, LANES)


def widen(ref, out_ref):
    width = ref.shape[0]
    out_ref[:width, :] = ref[...]
    out_ref[width:, :] = jnp.zeros((out_ref.shape[0] - width, out_ref.shape[1]), jnp.float32)


def select_columns(onehot, x, terms):
    total = None
    for part in split(x, terms):
        product = lax.dot_general(onehot, part, (((1,), (1,)), ((), ())), preferred_element_type=jnp.float32)
        total = product if total is None else total + product
    return total


def own_row(neg_ref, n):
    return neg_ref[0, 0, n // 2 : n // 2 + 1, n % 2 : n % 2 + 1]


def negs_kernel(neg_ref, table_ref, out_ref, table):
    widen(table_ref, table)
    entities = table.shape[1]
    place = lax.broadcasted_iota(jnp.int32, (8, entities), 0)
    entity = lax.broadcasted_iota(jnp.int32, (8, entities), 1)
    hit = jnp.zeros((8, entities), jnp.float32)
    for n in range(4):
        hit = jnp.where((place == n) & (entity == own_row(neg_ref, n)), 1.0, hit)
    rows = select_columns(hit.astype(jnp.bfloat16), table[...], 3)
    for j in range(CHUNKS - 1):
        part = rows[:4, j * LANES : (j + 1) * LANES]
        out_ref[:, j * 4 : j * 4 + 4, :] = jnp.broadcast_to(part, (out_ref.shape[0], 4, LANES))
    last = rows[:, (CHUNKS - 1) * LANES :]
    tail = last[:1]
    for n in range(1, 4):
        tail = tail + pltpu.roll(last, TAIL * n, 1)[n : n + 1]
    out_ref[:, UNIT - 1 : UNIT, :] = jnp.broadcast_to(tail, (out_ref.shape[0], 1, LANES))


def pick_kernel(send_ref, table_ref, rows_ref, table):
    widen(table_ref, table)
    onehot = onehot_of(send_ref[...], (send_ref.shape[0], table.shape[1]), 1)
    pack(select_columns(onehot, table[...], 3), rows_ref)


def grad_kernel(col_ref, row_ref, rel_ref, got_ref, negs_ref, back_ref, negs_back_ref, rows, negs, grads):
    unpack(got_ref, rows)
    slots, ends = rows.shape[0], col_ref.shape[0]
    edges = ends // 2
    blocks = rel_ref.shape[0]
    block = edges // blocks
    owners = negs_ref.shape[0] // UNIT
    tails = negs_ref[pl.ds(UNIT - 1, owners, stride=UNIT), :]
    live = lax.broadcasted_iota(jnp.int32, tails.shape, 1) < TAIL
    tail = jnp.zeros((owners, LANES), jnp.float32)
    picked = select_rows(onehot_of(col_ref[...], (ends, slots), 1), rows[...], 3)
    for c in range(blocks):
        for k in range(2):
            n = c * 2 + k
            for j in range(CHUNKS - 1):
                negs[c, k * owners : (k + 1) * owners, j * LANES : (j + 1) * LANES] = negs_ref[
                    pl.ds(j * 4 + n, owners, stride=UNIT), :
                ]
            turned = pltpu.roll(tails, LANES - TAIL * n, 1) if n else tails
            negs[c, k * owners : (k + 1) * owners, (CHUNKS - 1) * LANES :] = jnp.where(live, turned, 0.0)
    every = range(blocks)
    relation = [rel_ref[c : c + 1, :] for c in every]
    query = [picked[c * block : (c + 1) * block] * relation[c] for c in every]
    target = [picked[edges + c * block : edges + (c + 1) * block] for c in every]
    query_terms = [split(query[c], 3) for c in every]
    negative_terms = [split(negs[c], 3) for c in every]
    scores = [dot_terms(query_terms[c], negative_terms[c], ((1,), (1,)), FULL) for c in every]
    positive = [jnp.sum(query[c] * target[c], axis=1, keepdims=True) for c in every]
    largest = [jnp.maximum(jnp.max(scores[c], axis=1, keepdims=True), positive[c]) for c in every]
    pos_exp = [jnp.exp(positive[c] - largest[c]) for c in every]
    neg_exp = [jnp.exp(scores[c] - largest[c]) for c in every]
    total = [pos_exp[c] + jnp.sum(neg_exp[c], axis=1, keepdims=True) for c in every]
    pos_weight = [pos_exp[c] / total[c] - 1.0 for c in every]
    weight = [neg_exp[c] / total[c] for c in every]
    pulled = [dot_terms(split(weight[c], 2), negative_terms[c], ((1,), (0,)), NEAR) for c in every]
    pushed = [dot_terms(split(weight[c].T, 2), query_terms[c], ((1,), (0,)), NEAR) for c in every]
    for c in every:
        grads[c * block : (c + 1) * block, :] = (pos_weight[c] * target[c] + pulled[c]) * relation[c]
        grads[edges + c * block : edges + (c + 1) * block, :] = pos_weight[c] * query[c]
    for c in every:
        for k in range(2):
            n = c * 2 + k
            part = pushed[c][k * owners : (k + 1) * owners]
            for j in range(CHUNKS - 1):
                negs_back_ref[pl.ds(j * 4 + n, owners, stride=UNIT), :] = part[:, j * LANES : (j + 1) * LANES]
            last = part[:, (CHUNKS - 1) * LANES :]
            tail = tail + (pltpu.roll(last, TAIL * n, 1) if n else last)
    negs_back_ref[pl.ds(UNIT - 1, owners, stride=UNIT), :] = tail
    pack(select_rows(onehot_of(row_ref[...], (slots, ends), 0), grads[...], 2), back_ref)


def put_kernel(send_ref, got_ref, out_ref, rows):
    unpack(got_ref, rows)
    entities = out_ref.shape[1]
    out_ref[...] = select_rows(onehot_of(send_ref[...], (entities, rows.shape[0]), 0), rows[...], 2).T


def add_kernel(neg_ref, put_ref, parts_ref, out_ref, total, sems):
    own = jnp.sum(parts_ref[...], axis=0).T
    width, entities = out_ref.shape
    copies = []
    for j in range(CHUNKS):
        stop = min(width, (j + 1) * LANES) - j * LANES
        part = put_ref[j * LANES : j * LANES + stop, :]
        entity = lax.broadcasted_iota(jnp.int32, part.shape, 1)
        for n in range(4):
            if stop == LANES:
                own_part = own[:, j * 4 + n : j * 4 + n + 1]
            else:
                own_part = own[TAIL * n : TAIL * n + stop, UNIT - 1 : UNIT]
            part = part + jnp.where(entity == own_row(neg_ref, n), own_part, 0.0)
        rows = pl.ds(j * LANES, stop)
        total[rows, :] = part
        copies.append(pltpu.make_async_copy(total.at[rows], out_ref.at[rows], sems.at[j]))
        copies[-1].start()
    for copy in copies:
        copy.wait()


def near(x):
    return pltpu.with_memory_space_constraint(x, pltpu.VMEM)


def shaped(*shape):
    return jax.ShapeDtypeStruct(shape, jnp.float32)


def in_vmem(*shape):
    return pltpu.VMEM(shape, jnp.float32)


def quarters(columns):
    side = 1
    while side * side < columns:
        side *= 2
    depth = columns // side
    groups = [
        [y * side + z for y in range(top, top + depth // 2) for z in range(left, left + side // 2)]
        for top in (0, depth // 2)
        for left in (0, side // 2)
    ]

    def mirror(flip_y, flip_z):
        pairs = []
        for b in range(columns):
            y, z = divmod(b, side)
            pairs.append((b, (depth - 1 - y if flip_y else y) * side + (side - 1 - z if flip_z else z)))
        return pairs

    return groups, [mirror(False, True), mirror(True, False), mirror(True, True)]


def gather_columns(x, columns, later):
    groups, mirrors = quarters(columns)
    x = lax.all_to_all(x, "bucket", split_axis=0, concat_axis=0, axis_index_groups=groups, tiled=True)
    x, later = lax.optimization_barrier((x.reshape(len(groups[0]) * UNIT, LANES), later))
    return jnp.stack([x] + [lax.ppermute(x, "bucket", pairs) for pairs in mirrors]), later


def sum_columns(x, columns):
    groups, mirrors = quarters(columns)
    x = x.reshape(4, len(groups[0]) * UNIT, LANES)
    both, up, across = [lax.ppermute(x[i], "bucket", mirrors[i - 1]) for i in (3, 2, 1)]
    x = ((both + up) + across) + x[0]
    x = x.reshape(len(groups[0]), UNIT, LANES)
    return lax.all_to_all(x, "bucket", split_axis=0, concat_axis=0, axis_index_groups=groups, tiled=True)


def on_device(emb_table, rel_diag, send_rows, src_slot, dst_slot, neg_rows, block_rel):
    entities, width = emb_table.shape
    owners, slots = send_rows.shape[2:]
    columns = lax.axis_size("bucket")
    packed = (owners, (CHUNKS - 1) * slots + slots // 8, LANES)
    send = send_rows.reshape(owners * slots)
    table = emb_table.T
    own_negs = pl.pallas_call(
        negs_kernel,
        out_shape=shaped(columns // 4, UNIT, LANES),
        in_specs=[VMEM, VMEM],
        out_specs=VMEM,
        scratch_shapes=[in_vmem(WIDE, entities)],
        name="negs",
    )(neg_rows, table)
    picked = pl.pallas_call(
        pick_kernel,
        out_shape=shaped(*packed),
        in_specs=[VMEM, VMEM],
        out_specs=VMEM,
        scratch_shapes=[in_vmem(WIDE, entities)],
        name="pick",
    )(near(send[:, None]), near(table))
    negs, (sources, targets, kinds) = gather_columns(own_negs, columns, (src_slot, dst_slot, block_rel))
    got = lax.all_to_all(picked, "dom", split_axis=0, concat_axis=0, tiled=True)
    ends = jnp.concatenate([sources.reshape(-1), targets.reshape(-1)])
    relation = jnp.pad(rel_diag[kinds.reshape(-1)], ((0, 0), (0, WIDE - width)))
    back, negs_back = pl.pallas_call(
        grad_kernel,
        out_shape=(shaped(*packed), in_vmem(columns * UNIT, LANES)),
        in_specs=[VMEM] * 5,
        out_specs=(VMEM, VMEM),
        scratch_shapes=[
            in_vmem(owners * slots, WIDE),
            in_vmem(block_rel.shape[2], 2 * columns, WIDE),
            in_vmem(ends.shape[0], WIDE),
        ],
        name="grad",
    )(near(ends[:, None]), near(ends[None, :]), near(relation), near(got), near(negs.reshape(columns * UNIT, LANES)))
    own_grad = sum_columns(negs_back, columns)
    returned = lax.all_to_all(back, "dom", split_axis=0, concat_axis=0, tiled=True)
    put = pl.pallas_call(
        put_kernel,
        out_shape=in_vmem(WIDE, entities),
        in_specs=[VMEM, VMEM],
        out_specs=VMEM,
        scratch_shapes=[in_vmem(owners * slots, WIDE)],
        name="put",
    )(near(send[None, :]), near(returned))
    return pl.pallas_call(
        add_kernel,
        out_shape=shaped(width, entities),
        in_specs=[VMEM, VMEM, VMEM],
        out_specs=pl.BlockSpec(memory_space=pl.ANY),
        scratch_shapes=[in_vmem(width, entities), pltpu.SemaphoreType.DMA((CHUNKS,))],
        name="add",
    )(near(neg_rows), near(put), near(own_grad)).T


def solution(mesh):
    placed = (
        P(("dom", "bucket"), None),
        P(),
        P("dom", "bucket", None, None),
        P("dom", "bucket", None),
        P("dom", "bucket", None),
        P("dom", "bucket", None, None),
        P("dom", "bucket", None),
    )
    return jax.shard_map(
        on_device, mesh=mesh, in_specs=placed, out_specs=P(("dom", "bucket"), None), check_vma=False
    )
```
